32 devices in a mesh: elem: 8 (over z, y), gpt: 4 (over x, core).
Axes of the slice: x: 2, y: 2, z: 4, core: 2. Of those that a mesh axis runs over, the one named last changes fastest.
Arguments:
- slab_kelvin: float32 [16, 4096], P(None, 'elem'), may hold values from 190 to 310
- moisture_mass_load: float32 [16, 4096], P(None, 'elem'), may hold values from 0.1 to 1
- dioxide_mass_load: float32 [16, 4096], P(None, 'elem'), may hold values from 0.2 to 1
- slab_depth_share: float32 [16, 4096], P(None, 'elem'), may hold values from 0.01 to 0.06
- lower_node_slot: int32 [16, 4096], P(None, 'elem'), may hold values from 0 to 57
- upper_node_share: float32 [16, 4096], P(None, 'elem'), may hold values from 0 to 1
- ground_skin_kelvin: float32 [4096], P('elem'), may hold values from 230 to 310
- ground_reflectivity: float32 [4096], P('elem'), may hold values from 0.05 to 0.8
- sun_angle_class: int32 [4096], P('elem'), may hold values from 0 to 127, as said below
- owner_profile_routes: int32 [4096], P('elem'), may hold values from 0 to 511, as said below
- sunlit_angle_factors: float32 [64], replicated, may hold values from 0.05 to 1
- thermal_absorptivity: bfloat16 [128, 118], P('gpt'), may hold values from 0.0019989014 to 2
- sunlight_absorptivity: bfloat16 [112, 118], P('gpt'), may hold values from 0.0019989014 to 1
- emission_quadrature_share: float32 [128], P('gpt'), may hold values from 0.00390625 to 0.015625
- insolation_quadrature_share: float32 [112], P('gpt'), may hold values from 0.004464286 to 0.017857144
Outputs:
- heat_lw: float32 [16, 4096], P('gpt', 'elem')
- heat_sw: float32 [16, 4096], P('gpt', 'elem')
- surface_flux: float32 [4, 4096], P('gpt', 'elem')
The draws below stay inside these ranges and needn't reach their ends.
Inputs may be any that keep to these rules, and one draw needn't show every extreme that they name: `sun_angle_class`: A column is sunlit when its bin is below 64. Every span receives exactly 256 sunlit columns, and an owner gives equally many sunlit columns to every span. `owner_profile_routes`: for each owner, a permutation of its local column numbers 0 to 511.
All inputs are finite; a program needn't handle non-finite values.
Results may differ from the reference program's by a relative error of at most 0.0014.
Values may be sent and summed in bfloat16 or wider, within the bound.
No kernel may reach another device: no remote copies, remote signals or barrier semaphores. Data moves between devices by JAX's collectives and lax.ppermute only.
A program may use at most 64 MiB of HBM per device.

```python
import math
import jax
import jax.numpy as jnp
from jax import lax

G_LW = 128
G_SW = 112
NP = 59
SLAB_AMOUNT = 16
DAY_BINS = 64
COL_DEV = 512
PEER = 64
ALL_PROFILES = 4096
N_ELEM = 8


def sky_layout(key):
    base = jax.random.fold_in(key, 11)
    keys = jax.random.split(base, 5)
    per_peer = COL_DEV // N_ELEM
    owners = jnp.arange(N_ELEM, dtype=jnp.int32)
    turn = jax.random.randint(keys[0], (), 0, N_ELEM)
    split_at = jax.random.randint(keys[1], (), 0, per_peer + 1)
    place = (owners + turn) % N_ELEM
    middle = N_ELEM // 2
    sunny_share = jnp.where(place < middle - 1, per_peer, jnp.where(place == middle - 1, split_at, jnp.where(place == middle, per_peer - split_at, 0)))
    shuffled = jax.vmap(lambda sub_key: jax.random.permutation(sub_key, COL_DEV))(jax.random.split(keys[2], N_ELEM)).astype(jnp.int32)
    ranks = jnp.argsort(shuffled, axis=1)
    sunny_total = sunny_share * N_ELEM
    sunlit = ranks < sunny_total[:, None]
    spans = jnp.arange(N_ELEM, dtype=jnp.int32)[None, :, None]
    slots = jnp.arange(per_peer, dtype=jnp.int32)[None, None, :]
    share = sunny_share[:, None, None]
    pick = jnp.where(slots < share, spans * share + slots, sunny_total[:, None, None] + spans * (per_peer - share) + slots - share)
    base_order = jnp.take_along_axis(shuffled, pick.reshape(N_ELEM, COL_DEV), axis=1).reshape(N_ELEM, N_ELEM, per_peer)
    scores = jax.random.randint(keys[3], (N_ELEM, N_ELEM, per_peer), 0, 1 << 20) * per_peer + slots
    within = jnp.argsort(scores, axis=2)
    pack = jnp.take_along_axis(base_order, within, axis=2).reshape(-1).astype(jnp.int32)
    bins = jax.random.randint(keys[4], (N_ELEM, COL_DEV), 0, DAY_BINS) + jnp.where(sunlit, 0, DAY_BINS)
    return (bins.reshape(-1).astype(jnp.int32), pack)


def draw_sun_angle_class(key, part):
    return sky_layout(key)[0]


def draw_owner_profile_routes(key, part):
    return sky_layout(key)[1]


def with_ends(values, own_key, least, largest):
    extent = values.shape
    spot = [jax.random.randint(jax.random.fold_in(own_key, axis), (), 0, extent[axis]) for axis in range(len(extent))]
    values = values.at[tuple(spot)].set(least)
    longest = extent.index(max(extent))
    spot[longest] = (spot[longest] + 1) % extent[longest]
    return values.at[tuple(spot)].set(largest)


def levels(stream_key, dims, cuts, smallest, largest):
    factor_of = 1.0
    for axis_at, shards_of in cuts:
        steps = jax.random.uniform(jax.random.fold_in(jax.random.fold_in(stream_key, 6), axis_at), (shards_of,), jnp.float32, smallest / len(cuts), largest / len(cuts))
        factor_of = factor_of * jnp.repeat(jnp.exp(steps), dims[axis_at] // shards_of).reshape((-1,) + (1,) * (len(dims) - 1 - axis_at))
    return factor_of


def setup_inputs(seed: int = 0) -> dict:
    key_list = jax.random.split(jax.random.key(seed), 16)
    return {
        "slab_kelvin": jnp.clip(190.0 + 120.0 * jax.random.uniform(key_list[0], (SLAB_AMOUNT, ALL_PROFILES), jnp.float32) ** levels(key_list[0], (SLAB_AMOUNT, ALL_PROFILES), ((1, 8),), -0.2, 0.2), 190.0, 310.0),
        "moisture_mass_load": jnp.clip(jnp.exp(math.log(1.0) - 2.3025851 * jax.random.uniform(key_list[1], (SLAB_AMOUNT, ALL_PROFILES), jnp.float32) ** levels(key_list[1], (SLAB_AMOUNT, ALL_PROFILES), ((1, 8),), -0.2, 0.2)), 0.1, 1.0),
        "dioxide_mass_load": jnp.clip(jnp.exp(math.log(1.0) - 1.609438 * jax.random.uniform(key_list[2], (SLAB_AMOUNT, ALL_PROFILES), jnp.float32) ** levels(key_list[2], (SLAB_AMOUNT, ALL_PROFILES), ((1, 8),), -0.2, 0.2)), 0.2, 1.0),
        "slab_depth_share": jnp.clip(jnp.exp(math.log(0.06) - 1.7917595 * jax.random.uniform(key_list[3], (SLAB_AMOUNT, ALL_PROFILES), jnp.float32) ** levels(key_list[3], (SLAB_AMOUNT, ALL_PROFILES), ((1, 8),), -0.2, 0.2)), 0.01, 0.06),
        "lower_node_slot": with_ends(jax.random.randint(key_list[4], (SLAB_AMOUNT, ALL_PROFILES), 0, NP - 1), jax.random.fold_in(key_list[4], 1), 0, (NP - 1) - 1).astype(jnp.int32),
        "upper_node_share": jnp.clip(1.0 * jax.random.uniform(key_list[5], (SLAB_AMOUNT, ALL_PROFILES), jnp.float32) ** levels(key_list[5], (SLAB_AMOUNT, ALL_PROFILES), ((1, 8),), -0.2, 0.2), 0.0, 1.0),
        "ground_skin_kelvin": jnp.clip(230.0 + 80.0 * jax.random.uniform(key_list[6], (ALL_PROFILES,), jnp.float32) ** levels(key_list[6], (ALL_PROFILES,), ((0, 8),), -0.2, 0.2), 230.0, 310.0),
        "ground_reflectivity": jnp.clip(0.05 + 0.75 * jax.random.uniform(key_list[7], (ALL_PROFILES,), jnp.float32) ** levels(key_list[7], (ALL_PROFILES,), ((0, 8),), -0.2, 0.2), 0.05, 0.8),
        "sun_angle_class": draw_sun_angle_class(jax.random.fold_in(key_list[15], 71), 0),
        "owner_profile_routes": draw_owner_profile_routes(jax.random.fold_in(key_list[15], 71), 0),
        "sunlit_angle_factors": jnp.clip(jnp.exp(jax.random.uniform(key_list[10], (DAY_BINS,), jnp.float32, math.log(0.05), math.log(1.0))), 0.05, 1.0),
        "thermal_absorptivity": jnp.clip(jnp.exp(math.log(2.0) - 6.9083047 * jax.random.uniform(key_list[11], (G_LW, 2 * NP), jnp.float32) ** levels(key_list[11], (G_LW, 2 * NP), ((0, 4),), -0.2, 0.2)), 0.0019989014, 2.0).astype(jnp.bfloat16),
        "sunlight_absorptivity": jnp.clip(jnp.exp(math.log(1.0) - 6.2151576 * jax.random.uniform(key_list[12], (G_SW, 2 * NP), jnp.float32) ** levels(key_list[12], (G_SW, 2 * NP), ((0, 4),), -0.2, 0.2)), 0.0019989014, 1.0).astype(jnp.bfloat16),
        "emission_quadrature_share": jnp.clip(jnp.exp(math.log(0.015625) - 1.3862944 * jax.random.uniform(key_list[13], (G_LW,), jnp.float32) ** levels(key_list[13], (G_LW,), ((0, 4),), -0.2, 0.2)), 0.00390625, 0.015625),
        "insolation_quadrature_share": jnp.clip(jnp.exp(math.log(0.017857144) - 1.3862944 * jax.random.uniform(key_list[14], (G_SW,), jnp.float32) ** levels(key_list[14], (G_SW,), ((0, 4),), -0.2, 0.2)), 0.004464286, 0.017857144),
    }


def compose(earlier, later):
    return earlier[0] * later[0], later[0] * earlier[1] + later[1]


def zenith_cosine(bins, table):
    node_index = jnp.arange(table.shape[0], dtype=jnp.int32)[:, None]
    return jnp.sum(jnp.where(bins[None, :] == node_index, table[:, None], 0.0), axis=0)


def absorber(state_inputs, node_count):
    node_values = jnp.arange(node_count).astype(state_inputs.dtype)[:, None, None]
    node_index = state_inputs[4][None]
    weight = state_inputs[5][None]
    interp_weights = jnp.where(node_values == node_index, 1.0 - weight, 0.0) + jnp.where(node_values == node_index + 1.0, weight, 0.0)
    amount = jnp.concatenate([interp_weights * state_inputs[1][None], interp_weights * state_inputs[2][None]], axis=0).astype(jnp.bfloat16)
    return amount.reshape(2 * node_count, -1)


def longwave(tau, state_inputs, profile, planck):
    transmit = jnp.exp(-1.66 * tau)
    source = planck[:, None, None] * (state_inputs[0][None] / 250.0) ** 4
    emitted = source * (1.0 - transmit)
    downward = lax.associative_scan(compose, (transmit, emitted), axis=1)[1]
    rise_gain, rise_add = lax.associative_scan(compose, (transmit, emitted), axis=1, reverse=True)
    ground = planck[:, None] * (profile[0][None] / 250.0) ** 4
    up_top = rise_gain * ground[:, None, :] + rise_add
    up_bottom = jnp.concatenate([up_top[:, 1:], ground[:, None, :]], axis=1)
    down_top = jnp.concatenate([jnp.zeros_like(downward[:, :1]), downward[:, :-1]], axis=1)
    heating = jnp.sum((up_bottom - downward) - (up_top - down_top), axis=0) / state_inputs[3]
    return heating, jnp.sum(downward[:, -1], axis=0), jnp.sum(up_top[:, 0], axis=0)


def shortwave(tau, state_inputs, profile, solar):
    sun_height_factor = profile[2]
    safe_cosine = jnp.where(sun_height_factor > 0.0, sun_height_factor, 1.0)
    incident = solar[:, None] * sun_height_factor[None]
    direct_bottom = incident[:, None, :] * jnp.exp(-jnp.cumsum(tau / safe_cosine[None, None, :], axis=1))
    direct_top = jnp.concatenate([incident[:, None, :], direct_bottom[:, :-1]], axis=1)
    depth_below = jnp.flip(jnp.cumsum(jnp.flip(1.66 * tau, 1), axis=1), 1)
    ground = profile[1][None] * direct_bottom[:, -1]
    up_top = ground[:, None, :] * jnp.exp(-depth_below)
    up_bottom = jnp.concatenate([up_top[:, 1:], ground[:, None, :]], axis=1)
    heating = jnp.sum((direct_top - up_top) - (direct_bottom - up_bottom), axis=0) / state_inputs[3]
    return heating, jnp.sum(direct_bottom[:, -1], axis=0), jnp.sum(up_top[:, 0], axis=0)


def radiate(state_inputs, profile, thermal_absorptivity, sunlight_absorptivity, planck, solar):
    node_count = thermal_absorptivity.shape[1] // 2
    slab_heights = state_inputs.shape[1]
    profile_ordinal = state_inputs.shape[2]
    amount = absorber(state_inputs, node_count)
    tau_long = jnp.dot(thermal_absorptivity, amount, preferred_element_type=jnp.float32).reshape(thermal_absorptivity.shape[0], slab_heights, profile_ordinal)
    heat_long, down_ground, outgoing = longwave(tau_long, state_inputs, profile, planck)
    tau_short = jnp.dot(sunlight_absorptivity, amount, preferred_element_type=jnp.float32).reshape(sunlight_absorptivity.shape[0], slab_heights, profile_ordinal)
    heat_short, direct_ground, reflected = shortwave(tau_short, state_inputs, profile, solar)
    return jnp.stack([heat_long, heat_short], axis=1), jnp.stack([down_ground, outgoing, direct_ground, reflected], axis=0)


def reference(slab_kelvin, moisture_mass_load, dioxide_mass_load, slab_depth_share, lower_node_slot, upper_node_share, ground_skin_kelvin, ground_reflectivity, sun_angle_class, owner_profile_routes, sunlit_angle_factors, thermal_absorptivity, sunlight_absorptivity, emission_quadrature_share, insolation_quadrature_share):
    sun_height_factor = zenith_cosine(sun_angle_class, sunlit_angle_factors)
    state_inputs = jnp.stack([slab_kelvin, moisture_mass_load, dioxide_mass_load, slab_depth_share, lower_node_slot.astype(jnp.float32), upper_node_share])
    profile = jnp.stack([ground_skin_kelvin, ground_reflectivity, sun_height_factor])

    def one_block(block_start):
        field_part = lax.dynamic_slice_in_dim(state_inputs, block_start, COL_DEV, 2)
        side_part = lax.dynamic_slice_in_dim(profile, block_start, COL_DEV, 1)
        return radiate(field_part, side_part, thermal_absorptivity, sunlight_absorptivity, emission_quadrature_share, insolation_quadrature_share)

    heating, fluxes = lax.map(one_block, jnp.arange(N_ELEM, dtype=jnp.int32) * COL_DEV)
    heating = jnp.moveaxis(heating, 0, 2).reshape(SLAB_AMOUNT, 2, ALL_PROFILES)
    fluxes = jnp.moveaxis(fluxes, 0, 1).reshape(4, ALL_PROFILES)
    pack_grid = owner_profile_routes.reshape(N_ELEM, N_ELEM, PEER)
    global_cols = pack_grid + (jnp.arange(N_ELEM, dtype=jnp.int32) * COL_DEV)[:, None, None]
    span_cols = jnp.transpose(global_cols, (1, 0, 2)).reshape(-1).astype(jnp.int32)
    return heating[:, 0], heating[:, 1], fluxes[:, span_cols]
```

```python
import functools

import jax
import jax.numpy as jnp
from jax import lax
from jax.experimental import pallas as pl
from jax.experimental.pallas import tpu as pltpu
from jax.sharding import PartitionSpec as P

F32 = jnp.float32
BF16 = jnp.bfloat16
LANES = 128
LOG2E = 1.4426950408889634
DIFFUSE = -1.66 * LOG2E
BLOCK = 256


def up_to(count, step):
    return (count + step - 1) // step * step


def pick(row, index):
    blocks = row.shape[1] // LANES
    out = []
    for at in range(index.shape[1] // LANES):
        want = index[:, at * LANES : (at + 1) * LANES]
        inside = jnp.broadcast_to(want % LANES, (row.shape[0], LANES))
        got = None
        for b in range(blocks):
            piece = jnp.take_along_axis(row[:, b * LANES : (b + 1) * LANES], inside, axis=1, mode="promise_in_bounds")
            got = piece if b == 0 else jnp.where(want // LANES == b, piece, got)
        out.append(got)
    return jnp.concatenate(out, axis=1)


def column_of(row, rows, count):
    if count < rows:
        row = jnp.concatenate([row, jnp.zeros((1, rows - count), row.dtype)], axis=1)
    across = lax.broadcasted_iota(jnp.int32, (rows, rows), 1)
    down = lax.broadcasted_iota(jnp.int32, (rows, rows), 0)
    square = jnp.where(across == down, jnp.broadcast_to(row, (rows, rows)), 0.0)
    return jnp.sum(square, axis=1, keepdims=True)


def fold(x):
    out = x[:8]
    for r in range(8, x.shape[0], 8):
        out = out + x[r : r + 8]
    return out


def column_kernel(
    kelvin_ref,
    moist_ref,
    diox_ref,
    depth_ref,
    slot_ref,
    share_ref,
    skin_ref,
    albedo_ref,
    sun_ref,
    routes_ref,
    angles_ref,
    thermal_ref,
    sunlight_ref,
    planck_ref,
    solar_ref,
    *rest,
    elem_size,
    group_size,
):
    heat_refs = rest[:group_size]
    flux_ref = rest[group_size]
    table, tau, part, heat, rows_node, rows_ml, rows_mu, rows_dl, rows_du, warm = rest[group_size + 1 :]
    layers, columns = kelvin_ref.shape
    lw, terms = thermal_ref.shape
    sw = sunlight_ref.shape[0]
    nodes = terms // 2
    lw_rows, sw_rows, node_rows = up_to(lw, 16), up_to(sw, 16), up_to(nodes, 16)
    me_elem, me_gpt = lax.axis_index("elem"), lax.axis_index("gpt")

    table[...] = jnp.zeros_like(table)
    for first, ref, count in ((0, thermal_ref, lw), (lw_rows, sunlight_ref, sw)):
        values = ref[...]
        table[first : first + count, 0:nodes] = values[:, :nodes]
        table[first : first + count, node_rows : node_rows + nodes] = values[:, nodes:]

    share = share_ref[...]
    rows_node[...] = slot_ref[...].astype(F32)
    rows_ml[...] = (1.0 - share) * moist_ref[...]
    rows_mu[...] = share * moist_ref[...]
    rows_dl[...] = (1.0 - share) * diox_ref[...]
    rows_du[...] = share * diox_ref[...]
    relative = kelvin_ref[...] * (1.0 / 250.0)
    warm[...] = (relative * relative) * (relative * relative)

    node_of_row = lax.broadcasted_iota(jnp.int32, (node_rows, columns), 0).astype(F32).astype(BF16)
    zero = jnp.zeros((node_rows, columns), BF16)

    def spread(ref, l):
        row = jnp.broadcast_to(ref[pl.ds(l, 1), :], (16, columns)).astype(BF16)
        return jnp.concatenate([row] * (node_rows // 16), axis=0)

    def depths(l, _):
        node = spread(rows_node, l)
        lower = node_of_row == node
        upper = node_of_row == node + jnp.asarray(1.0, BF16)
        wet = jnp.where(lower, spread(rows_ml, l), jnp.where(upper, spread(rows_mu, l), zero))
        dry = jnp.where(lower, spread(rows_dl, l), jnp.where(upper, spread(rows_du, l), zero))
        amount = jnp.concatenate([wet, dry], axis=0)
        tau[l] = jnp.dot(table[...], amount, preferred_element_type=F32)
        return _

    lax.fori_loop(0, layers, depths, 0, unroll=2)

    planck = jnp.broadcast_to(column_of(planck_ref[...].reshape(1, lw), lw_rows, lw), (lw_rows, BLOCK))
    solar = jnp.broadcast_to(column_of(solar_ref[...].reshape(1, sw), sw_rows, sw), (sw_rows, BLOCK))
    angles = angles_ref[...].reshape(1, angles_ref.shape[0])
    bins = angles.shape[1]
    if bins < LANES:
        angles = jnp.concatenate([angles, jnp.zeros((1, LANES - bins), F32)], axis=1)
    sun = sun_ref[...].reshape(1, columns)
    angles = jnp.broadcast_to(angles, (8, angles.shape[1]))
    cosine = jnp.where(sun < bins, pick(angles, jnp.minimum(sun, angles.shape[1] - 1))[:1], 0.0)
    skin = skin_ref[...].reshape(1, columns) * (1.0 / 250.0)
    skin = (skin * skin) * (skin * skin)
    albedo = albedo_ref[...].reshape(1, columns)
    slant = (-LOG2E) / jnp.where(cosine > 0.0, cosine, 1.0)

    flux_parts = []
    for first in range(0, columns, BLOCK):
        at = pl.ds(first, BLOCK)
        slant_here = slant[:, first : first + BLOCK]

        def fall(l, carry):
            down, beam = carry
            absorbed = 1.0 - jnp.exp2(DIFFUSE * tau[l, 0:lw_rows, at])
            tau[l, 0:lw_rows, at] = absorbed
            gain = absorbed * (down - warm[pl.ds(l, 1), at])
            part[0, l, :, at] = fold(gain * planck)
            passed = beam * jnp.exp2(slant_here * tau[l, lw_rows : lw_rows + sw_rows, at])
            part[1, l, :, at] = fold((beam - passed) * solar)
            return down - gain, passed

        down, beam = lax.fori_loop(
            0,
            layers,
            fall,
            (jnp.zeros((lw_rows, BLOCK), F32), jnp.ones((sw_rows, BLOCK), F32)),
            unroll=2,
        )
        up = jnp.broadcast_to(skin[:, first : first + BLOCK], (lw_rows, BLOCK))
        back = albedo[:, first : first + BLOCK] * beam

        def rise(i, carry):
            l = layers - 1 - i
            up, back = carry
            gain = tau[l, 0:lw_rows, at] * (up - warm[pl.ds(l, 1), at])
            part[0, l, :, at] += fold(gain * planck)
            passed = back * jnp.exp2(DIFFUSE * tau[l, lw_rows : lw_rows + sw_rows, at])
            part[1, l, :, at] += fold((back - passed) * solar)
            return up - gain, passed

        up, back = lax.fori_loop(0, layers, rise, (up, back), unroll=2)
        flux_parts.append([fold(down * planck), fold(up * planck), fold(beam * solar), fold(back * solar)])

    per = layers // group_size
    inverse = 1.0 / depth_ref[...]
    for kind, scale in ((0, inverse), (1, inverse * cosine)):
        for l in range(layers):
            row = jnp.sum(part[kind, l], axis=0, keepdims=True)
            heat[l // per, kind * per + l % per : kind * per + l % per + 1, :] = row * scale[l : l + 1]
    for d in range(group_size):
        heat_refs[d][...] = heat[jnp.bitwise_xor(me_gpt, d)]

    rows = []
    for i, scale in enumerate((1.0, 1.0, cosine, cosine)):
        row = jnp.concatenate([jnp.sum(p[i], axis=0, keepdims=True) for p in flux_parts], axis=1)
        rows.append(row * scale)
    fluxes = jnp.concatenate(rows + [jnp.zeros((4, columns), F32)], axis=0)
    routed = pick(fluxes, routes_ref[...].reshape(1, columns))
    peer = columns // elem_size
    share_count = LANES // peer
    lane = lax.broadcasted_iota(jnp.int32, (8, LANES), 1)
    mine = lane // peer == lax.rem(me_elem, share_count)
    for k in range(elem_size):
        block = routed[:, k // share_count * LANES : (k // share_count + 1) * LANES]
        shift = lax.rem(me_elem + (elem_size * share_count - k), share_count) * peer
        moved = jnp.where(mine, pltpu.roll(block, shift, 1), 0.0)
        for q in range(group_size):
            flux_ref[k * group_size + q] = moved[q : q + 1]


def sum_kernel(*refs, group_size):
    heats = refs[:group_size]
    flux_ref, lw_ref, sw_ref, out_ref = refs[group_size:]
    total = heats[0][...]
    for ref in heats[1:]:
        total = total + ref[...]
    per = lw_ref.shape[0]
    lw_ref[...] = total[:per]
    sw_ref[...] = total[per:]
    blocks = out_ref.shape[1] // LANES
    count = flux_ref.shape[0] // blocks
    for b in range(blocks):
        piece = flux_ref[b * count : (b + 1) * count].reshape(count, LANES)
        out_ref[:, b * LANES : (b + 1) * LANES] = jnp.sum(piece, axis=0, keepdims=True)


def local(*args):
    layers, columns = args[0].shape
    lw, terms = args[11].shape
    sw = args[12].shape[0]
    group_size, elem_size = lax.axis_size("gpt"), lax.axis_size("elem")
    lw_rows, sw_rows, node_rows = up_to(lw, 16), up_to(sw, 16), up_to(terms // 2, 16)
    per = layers // group_size
    vmem = pl.BlockSpec(memory_space=pltpu.VMEM)
    field = pltpu.VMEM((layers, columns), F32)
    *heats, flux = pl.pallas_call(
        functools.partial(column_kernel, elem_size=elem_size, group_size=group_size),
        out_shape=[jax.ShapeDtypeStruct((2 * per, columns), F32)] * group_size
        + [jax.ShapeDtypeStruct((elem_size * group_size, 1, LANES), F32)],
        in_specs=[vmem] * len(args),
        out_specs=[vmem] * (group_size + 1),
        scratch_shapes=[
            pltpu.VMEM((lw_rows + sw_rows, 2 * node_rows), BF16),
            pltpu.VMEM((layers, lw_rows + sw_rows, columns), F32),
            pltpu.VMEM((2, layers, 8, columns), F32),
            pltpu.VMEM((group_size, 2 * per, columns), F32),
            field,
            field,
            field,
            field,
            field,
            field,
        ],
        name="columns",
    )(*args)
    moved = [heats[0]]
    for d in range(1, group_size):
        moved.append(lax.ppermute(heats[d], "gpt", [(i, i ^ d) for i in range(group_size)]))
    flux = lax.all_to_all(flux, ("elem", "gpt"), 0, 0, tiled=True)
    return tuple(
        pl.pallas_call(
            functools.partial(sum_kernel, group_size=group_size),
            out_shape=[
                jax.ShapeDtypeStruct((per, columns), F32),
                jax.ShapeDtypeStruct((per, columns), F32),
                jax.ShapeDtypeStruct((1, columns), F32),
            ],
            in_specs=[vmem] * (group_size + 1),
            out_specs=[vmem] * 3,
            name="sums",
        )(*moved, flux)
    )


def solution(mesh):
    in_specs = (P(None, "elem"),) * 6 + (P("elem"),) * 4 + (P(), P("gpt", None), P("gpt", None), P("gpt"), P("gpt"))
    out_specs = (P("gpt", "elem"), P("gpt", "elem"), P("gpt", "elem"))
    return jax.shard_map(local, mesh=mesh, in_specs=in_specs, out_specs=out_specs, check_vma=False)
```

```python
import functools

import jax
import jax.numpy as jnp
from jax import lax
from jax.experimental import pallas as pl
from jax.experimental.pallas import tpu as pltpu
from jax.sharding import PartitionSpec as P

F32 = jnp.float32
BF16 = jnp.bfloat16
LANES = 128
LOG2E = 1.4426950408889634
DIFFUSE = -1.66 * LOG2E
BLOCK = 256


def up_to(count, step):
    return (count + step - 1) // step * step


def pick(row, index):
    blocks = row.shape[1] // LANES
    out = []
    for at in range(index.shape[1] // LANES):
        want = index[:, at * LANES : (at + 1) * LANES]
        inside = jnp.broadcast_to(want % LANES, (row.shape[0], LANES))
        got = None
        for b in range(blocks):
            piece = jnp.take_along_axis(row[:, b * LANES : (b + 1) * LANES], inside, axis=1, mode="promise_in_bounds")
            got = piece if b == 0 else jnp.where(want // LANES == b, piece, got)
        out.append(got)
    return jnp.concatenate(out, axis=1)


def column_of(row, rows, count):
    if count < rows:
        row = jnp.concatenate([row, jnp.zeros((1, rows - count), row.dtype)], axis=1)
    across = lax.broadcasted_iota(jnp.int32, (rows, rows), 1)
    down = lax.broadcasted_iota(jnp.int32, (rows, rows), 0)
    square = jnp.where(across == down, jnp.broadcast_to(row, (rows, rows)), 0.0)
    return jnp.sum(square, axis=1, keepdims=True)


def total(x, weights):
    x = x * weights
    out = x[:8]
    for r in range(8, x.shape[0], 8):
        out = out + x[r : r + 8]
    return jnp.sum(out, axis=0, keepdims=True)


def column_kernel(*refs, count, elem_size, group_size):
    ins, refs = refs[:count], refs[count:]
    kelvin_ref, moist_ref, diox_ref, depth_ref, slot_ref, share_ref, skin_ref, albedo_ref = ins[:8]
    sun_ref, routes_ref, angles_ref, thermal_ref, sunlight_ref, planck_ref, solar_ref = ins[8:]
    heat_refs, flux_ref, refs = refs[:group_size], refs[group_size], refs[group_size + 1 :]
    table, weights, passing, depths, falls, gains, heat, rows, warm, edge, sides, fluxes = refs
    layers, columns = kelvin_ref.shape
    lw, terms = thermal_ref.shape
    sw = sunlight_ref.shape[0]
    nodes = terms // 2
    lw_rows, sw_rows, node_rows = up_to(lw, 16), up_to(sw, 16), up_to(nodes, 16)
    both = lw_rows + sw_rows
    per = layers // group_size
    me_elem, me_gpt = lax.axis_index("elem"), lax.axis_index("gpt")

    table[...] = jnp.zeros_like(table)
    for first, ref, size in ((0, thermal_ref, lw), (lw_rows, sunlight_ref, sw)):
        values = ref[...]
        for kind in range(2):
            here = values[:, kind * nodes : (kind + 1) * nodes]
            at = kind * node_rows
            table[first : first + size, at : at + nodes] = here
            at = (2 + kind) * node_rows
            table[first : first + size, at : at + nodes - 1] = here[:, 1:]

    planck_row = planck_ref[...].reshape(1, lw)
    solar_row = solar_ref[...].reshape(1, sw)
    pieces = [planck_row, jnp.zeros((1, lw_rows - lw), F32), solar_row, jnp.zeros((1, sw_rows - sw), F32)]
    shares = jnp.concatenate([p for p in pieces if p.shape[1]] * per, axis=1)
    shares = jnp.broadcast_to(shares, (2 * per, per * both))
    lane = lax.broadcasted_iota(jnp.int32, shares.shape, 1)
    wanted = lax.div(lane, both) + jnp.where(lax.rem(lane, both) < lw_rows, 0, per)
    shares = jnp.where(lax.broadcasted_iota(jnp.int32, shares.shape, 0) == wanted, shares, 0.0)
    high = shares.astype(BF16).astype(F32)
    weights[...] = jnp.concatenate([high, shares - high], axis=0).astype(BF16)
    planck = column_of(planck_row, lw_rows, lw)
    solar = column_of(solar_row, sw_rows, sw)

    share = share_ref[...]
    rows[0] = slot_ref[...].astype(F32)
    rows[1] = (1.0 - share) * moist_ref[...]
    rows[2] = (1.0 - share) * diox_ref[...]
    rows[3] = share * moist_ref[...]
    rows[4] = share * diox_ref[...]
    relative = kelvin_ref[...] * (1.0 / 250.0)
    relative = relative * relative
    relative = relative * relative
    warm[...] = relative
    edge[0 : layers - 1] = relative[: layers - 1] - relative[1:]
    edge[layers - 1 : layers] = relative[layers - 1 :]

    angles = angles_ref[...].reshape(1, angles_ref.shape[0])
    bins = angles.shape[1]
    if bins % LANES:
        angles = jnp.concatenate([angles, jnp.zeros((1, up_to(bins, LANES) - bins), F32)], axis=1)
    sun = sun_ref[...].reshape(1, columns)
    angles = jnp.broadcast_to(angles, (8, angles.shape[1]))
    cosine = jnp.where(sun < bins, pick(angles, jnp.minimum(sun, angles.shape[1] - 1))[:1], 0.0)
    skin = skin_ref[...].reshape(1, columns) * (1.0 / 250.0)
    skin = skin * skin
    sides[0:1] = skin * skin
    sides[1:2] = albedo_ref[...].reshape(1, columns)
    sides[2:3] = (-LOG2E) / jnp.where(cosine > 0.0, cosine, 1.0)

    node_of_row = lax.broadcasted_iota(jnp.int32, (node_rows, BLOCK), 0).astype(F32).astype(BF16)
    zero = jnp.zeros((node_rows, BLOCK), BF16)

    def block(i, _):
        at = pl.ds(pl.multiple_of(i * BLOCK, BLOCK), BLOCK)

        def spread(kind, l):
            row = jnp.broadcast_to(rows[kind, l : l + 1, at], (16, BLOCK)).astype(BF16)
            return jnp.concatenate([row] * (node_rows // 16), axis=0)

        slant = sides[2:3, at]
        down = jnp.broadcast_to(-warm[0:1, at], (lw_rows, BLOCK))
        beam = jnp.ones((sw_rows, BLOCK), F32)
        for l in range(layers):
            here = node_of_row == spread(0, l)
            amount = jnp.concatenate([jnp.where(here, spread(kind, l), zero) for kind in range(1, 5)], axis=0)
            tau = jnp.dot(table[...], amount, preferred_element_type=F32)
            through = jnp.exp2(DIFFUSE * tau[:lw_rows])
            passed = through * down
            passing[l] = through
            falls[l, :lw_rows] = down - passed
            down = passed + edge[l : l + 1, at]
            tau = tau[lw_rows:]
            depths[l] = tau
            passed = beam * jnp.exp2(slant * tau)
            falls[l, lw_rows:] = beam - passed
            beam = passed
        up = sides[0:1, at] - warm[layers - 1 : layers, at]
        up = jnp.broadcast_to(up, (lw_rows, BLOCK))
        back = sides[1:2, at] * beam
        fluxes[0:1, at] = total(down, planck)
        fluxes[2:3, at] = total(beam, solar)
        for l in reversed(range(layers)):
            first = l % per * both
            passed = passing[l] * up
            gains[l // per, first : first + lw_rows] = ((up - passed) + falls[l, :lw_rows]).astype(BF16)
            up = passed - edge[l - 1 : l, at] if l else passed + warm[0:1, at]
            passed = back * jnp.exp2(DIFFUSE * depths[l])
            gains[l // per, first + lw_rows : first + both] = ((back - passed) + falls[l, lw_rows:]).astype(BF16)
            back = passed
            if l % per == 0:
                sums = jnp.dot(weights[...], gains[l // per], preferred_element_type=F32)
                heat[l // per, :, at] = sums[: 2 * per] + sums[2 * per :]
        fluxes[1:2, at] = total(up, planck)
        fluxes[3:4, at] = total(back, solar)
        return _

    lax.fori_loop(0, columns // BLOCK, block, 0)

    inverse = 1.0 / depth_ref[...]
    for q in range(group_size):
        scale = inverse[q * per : (q + 1) * per]
        heat[q] = heat[q] * jnp.concatenate([scale, scale * cosine], axis=0)
    for d in range(group_size):
        heat_refs[d][...] = heat[jnp.bitwise_xor(me_gpt, d)]

    row = lax.broadcasted_iota(jnp.int32, (8, columns), 0)
    routed = pick(fluxes[...] * jnp.where(row < 2, 1.0, cosine), routes_ref[...].reshape(1, columns))
    peer = columns // elem_size
    share_count = LANES // peer
    lane = lax.broadcasted_iota(jnp.int32, (8, LANES), 1)
    mine = lane // peer == lax.rem(me_elem, share_count)
    for k in range(elem_size):
        piece = routed[:, k // share_count * LANES : (k // share_count + 1) * LANES]
        shift = lax.rem(me_elem + (elem_size * share_count - k), share_count) * peer
        moved = jnp.where(mine, pltpu.roll(piece, shift, 1), 0.0)
        for q in range(group_size):
            flux_ref[k * group_size + q] = moved[q : q + 1]


def sum_kernel(*refs, group_size):
    heats = refs[:group_size]
    flux_ref, lw_ref, sw_ref, out_ref = refs[group_size:]
    total = heats[0][...]
    for ref in heats[1:]:
        total = total + ref[...]
    per = lw_ref.shape[0]
    lw_ref[...] = total[:per]
    sw_ref[...] = total[per:]
    blocks = out_ref.shape[1] // LANES
    count = flux_ref.shape[0] // blocks
    for b in range(blocks):
        piece = flux_ref[b * count : (b + 1) * count].reshape(count, LANES)
        out_ref[:, b * LANES : (b + 1) * LANES] = jnp.sum(piece, axis=0, keepdims=True)


def local(*args):
    layers, columns = args[0].shape
    lw, terms = args[11].shape
    sw = args[12].shape[0]
    group_size, elem_size = lax.axis_size("gpt"), lax.axis_size("elem")
    lw_rows, sw_rows, node_rows = up_to(lw, 16), up_to(sw, 16), up_to(terms // 2, 16)
    per = layers // group_size
    both = lw_rows + sw_rows
    vmem = pl.BlockSpec(memory_space=pltpu.VMEM)
    *heats, flux = pl.pallas_call(
        functools.partial(column_kernel, count=len(args), elem_size=elem_size, group_size=group_size),
        out_shape=[jax.ShapeDtypeStruct((2 * per, columns), F32)] * group_size
        + [jax.ShapeDtypeStruct((elem_size * group_size, 1, LANES), F32)],
        in_specs=[vmem] * len(args),
        out_specs=[vmem] * (group_size + 1),
        scratch_shapes=[
            pltpu.VMEM((both, 4 * node_rows), BF16),
            pltpu.VMEM((4 * per, per * both), BF16),
            pltpu.VMEM((layers, lw_rows, BLOCK), F32),
            pltpu.VMEM((layers, sw_rows, BLOCK), F32),
            pltpu.VMEM((layers, both, BLOCK), F32),
            pltpu.VMEM((group_size, per * both, BLOCK), BF16),
            pltpu.VMEM((group_size, 2 * per, columns), F32),
            pltpu.VMEM((5, layers, columns), F32),
            pltpu.VMEM((layers, columns), F32),
            pltpu.VMEM((layers, columns), F32),
            pltpu.VMEM((8, columns), F32),
            pltpu.VMEM((8, columns), F32),
        ],
        name="columns",
    )(*args)
    moved = [heats[0]]
    for d in range(1, group_size):
        moved.append(lax.ppermute(heats[d], "gpt", [(i, i ^ d) for i in range(group_size)]))
    flux = lax.all_to_all(flux, ("elem", "gpt"), 0, 0, tiled=True)
    return tuple(
        pl.pallas_call(
            functools.partial(sum_kernel, group_size=group_size),
            out_shape=[
                jax.ShapeDtypeStruct((per, columns), F32),
                jax.ShapeDtypeStruct((per, columns), F32),
                jax.ShapeDtypeStruct((1, columns), F32),
            ],
            in_specs=[vmem] * (group_size + 1),
            out_specs=[vmem] * 3,
            compiler_params=pltpu.CompilerParams(vmem_limit_bytes=2 << 20),
            name="sums",
        )(*moved, flux)
    )


def solution(mesh):
    in_specs = (P(None, "elem"),) * 6 + (P("elem"),) * 4 + (P(), P("gpt", None), P("gpt", None), P("gpt"), P("gpt"))
    out_specs = (P("gpt", "elem"), P("gpt", "elem"), P("gpt", "elem"))
    return jax.shard_map(local, mesh=mesh, in_specs=in_specs, out_specs=out_specs, check_vma=False)
```

```python
import functools

import jax
import jax.numpy as jnp
from jax import lax
from jax.experimental import pallas as pl
from jax.experimental.pallas import tpu as pltpu
from jax.sharding import PartitionSpec as P

F32 = jnp.float32
BF16 = jnp.bfloat16
LANES = 128
LOG2E = 1.4426950408889634
DIFFUSE = -1.66 * LOG2E
BLOCK = 512


def up_to(count, step):
    return (count + step - 1) // step * step


def pick(row, index):
    blocks = row.shape[1] // LANES
    out = []
    for at in range(index.shape[1] // LANES):
        want = index[:, at * LANES : (at + 1) * LANES]
        inside = jnp.broadcast_to(want % LANES, (row.shape[0], LANES))
        got = None
        for b in range(blocks):
            piece = jnp.take_along_axis(row[:, b * LANES : (b + 1) * LANES], inside, axis=1, mode="promise_in_bounds")
            got = piece if b == 0 else jnp.where(want // LANES == b, piece, got)
        out.append(got)
    return jnp.concatenate(out, axis=1)


def column_of(row, rows, count):
    if count < rows:
        row = jnp.concatenate([row, jnp.zeros((1, rows - count), row.dtype)], axis=1)
    across = lax.broadcasted_iota(jnp.int32, (rows, rows), 1)
    down = lax.broadcasted_iota(jnp.int32, (rows, rows), 0)
    square = jnp.where(across == down, jnp.broadcast_to(row, (rows, rows)), 0.0)
    return jnp.sum(square, axis=1, keepdims=True)


def total(x, weights):
    x = x * weights
    out = x[:8]
    for r in range(8, x.shape[0], 8):
        out = out + x[r : r + 8]
    return jnp.sum(out, axis=0, keepdims=True)


def column_kernel(*refs, count, elem_size, group_size):
    ins, refs = refs[:count], refs[count:]
    kelvin_ref, moist_ref, diox_ref, depth_ref, slot_ref, share_ref, skin_ref, albedo_ref = ins[:8]
    sun_ref, routes_ref, angles_ref, thermal_ref, sunlight_ref, planck_ref, solar_ref = ins[8:]
    heat_refs, flux_ref, refs = refs[:group_size], refs[group_size], refs[group_size + 1 :]
    table, weights, passing, depths, gains, heat, rows, warm, edge, sides, fluxes = refs
    layers, columns = kelvin_ref.shape
    lw, terms = thermal_ref.shape
    sw = sunlight_ref.shape[0]
    nodes = terms // 2
    lw_rows, sw_rows, node_rows = up_to(lw, 16), up_to(sw, 16), up_to(nodes, 16)
    both = lw_rows + sw_rows
    per = layers // group_size
    me_elem, me_gpt = lax.axis_index("elem"), lax.axis_index("gpt")

    table[...] = jnp.zeros_like(table)
    for first, ref, size in ((0, thermal_ref, lw), (lw_rows, sunlight_ref, sw)):
        values = ref[...]
        for kind in range(2):
            here = values[:, kind * nodes : (kind + 1) * nodes]
            at = kind * node_rows
            table[first : first + size, at : at + nodes] = here
            at = (2 + kind) * node_rows
            table[first : first + size, at : at + nodes - 1] = here[:, 1:]

    planck_row = planck_ref[...].reshape(1, lw)
    solar_row = solar_ref[...].reshape(1, sw)
    pieces = [planck_row, jnp.zeros((1, lw_rows - lw), F32), solar_row, jnp.zeros((1, sw_rows - sw), F32)]
    shares = jnp.concatenate([p for p in pieces if p.shape[1]] * per, axis=1)
    shares = jnp.broadcast_to(shares, (2 * per, per * both))
    lane = lax.broadcasted_iota(jnp.int32, shares.shape, 1)
    wanted = lax.div(lane, both) + jnp.where(lax.rem(lane, both) < lw_rows, 0, per)
    shares = jnp.where(lax.broadcasted_iota(jnp.int32, shares.shape, 0) == wanted, shares, 0.0)
    high = shares.astype(BF16).astype(F32)
    both_parts = jnp.concatenate([high, shares - high], axis=0).astype(BF16)
    weights[...] = jnp.concatenate([both_parts, both_parts], axis=1)
    planck = column_of(planck_row, lw_rows, lw)
    solar = column_of(solar_row, sw_rows, sw)

    share = share_ref[...]
    rows[0] = slot_ref[...].astype(F32)
    rows[1] = (1.0 - share) * moist_ref[...]
    rows[2] = (1.0 - share) * diox_ref[...]
    rows[3] = share * moist_ref[...]
    rows[4] = share * diox_ref[...]
    relative = kelvin_ref[...] * (1.0 / 250.0)
    relative = relative * relative
    relative = relative * relative
    warm[...] = relative
    edge[0 : layers - 1] = relative[: layers - 1] - relative[1:]
    edge[layers - 1 : layers] = relative[layers - 1 :]

    angles = angles_ref[...].reshape(1, angles_ref.shape[0])
    bins = angles.shape[1]
    if bins % LANES:
        angles = jnp.concatenate([angles, jnp.zeros((1, up_to(bins, LANES) - bins), F32)], axis=1)
    sun = sun_ref[...].reshape(1, columns)
    angles = jnp.broadcast_to(angles, (8, angles.shape[1]))
    cosine = jnp.where(sun < bins, pick(angles, jnp.minimum(sun, angles.shape[1] - 1))[:1], 0.0)
    skin = skin_ref[...].reshape(1, columns) * (1.0 / 250.0)
    skin = skin * skin
    sides[0:1] = skin * skin
    sides[1:2] = albedo_ref[...].reshape(1, columns)
    sides[2:3] = (-LOG2E) / jnp.where(cosine > 0.0, cosine, 1.0)

    node_of_row = lax.broadcasted_iota(jnp.int32, (node_rows, BLOCK), 0).astype(F32).astype(BF16)
    zero = jnp.zeros((node_rows, BLOCK), BF16)

    def block(i, _):
        at = pl.ds(pl.multiple_of(i * BLOCK, BLOCK), BLOCK)

        def spread(kind, l):
            row = jnp.broadcast_to(rows[kind, l : l + 1, at], (16, BLOCK)).astype(BF16)
            return jnp.concatenate([row] * (node_rows // 16), axis=0)

        slant = sides[2:3, at]
        down = jnp.broadcast_to(-warm[0:1, at], (lw_rows, BLOCK))
        beam = jnp.ones((sw_rows, BLOCK), F32)
        for l in range(layers):
            here = node_of_row == spread(0, l)
            amount = jnp.concatenate([jnp.where(here, spread(kind, l), zero) for kind in range(1, 5)], axis=0)
            tau = jnp.dot(table[...], amount, preferred_element_type=F32)
            through = jnp.exp2(DIFFUSE * tau[:lw_rows])
            passed = through * down
            passing[l] = through
            first = l % per * both
            gains[0, l // per, first : first + lw_rows] = (down - passed).astype(BF16)
            down = passed + edge[l : l + 1, at]
            tau = tau[lw_rows:]
            depths[l] = tau
            passed = beam * jnp.exp2(slant * tau)
            gains[0, l // per, first + lw_rows : first + both] = (beam - passed).astype(BF16)
            beam = passed
        up = sides[0:1, at] - warm[layers - 1 : layers, at]
        up = jnp.broadcast_to(up, (lw_rows, BLOCK))
        back = sides[1:2, at] * beam
        fluxes[0:1, at] = total(down, planck)
        fluxes[2:3, at] = total(beam, solar)
        for l in reversed(range(layers)):
            first = l % per * both
            passed = passing[l] * up
            gains[1, l // per, first : first + lw_rows] = (up - passed).astype(BF16)
            up = passed - edge[l - 1 : l, at] if l else passed + warm[0:1, at]
            passed = back * jnp.exp2(DIFFUSE * depths[l])
            gains[1, l // per, first + lw_rows : first + both] = (back - passed).astype(BF16)
            back = passed
            if l % per == 0:
                pair = jnp.concatenate([gains[0, l // per], gains[1, l // per]], axis=0)
                sums = jnp.dot(weights[...], pair, preferred_element_type=F32)
                heat[l // per, :, at] = sums[: 2 * per] + sums[2 * per :]
        fluxes[1:2, at] = total(up, planck)
        fluxes[3:4, at] = total(back, solar)
        return _

    lax.fori_loop(0, columns // BLOCK, block, 0)

    inverse = 1.0 / depth_ref[...]
    for q in range(group_size):
        scale = inverse[q * per : (q + 1) * per]
        heat[q] = heat[q] * jnp.concatenate([scale, scale * cosine], axis=0)
    for d in range(group_size):
        heat_refs[d][...] = heat[jnp.bitwise_xor(me_gpt, d)]

    row = lax.broadcasted_iota(jnp.int32, (8, columns), 0)
    routed = pick(fluxes[...] * jnp.where(row < 2, 1.0, cosine), routes_ref[...].reshape(1, columns))
    peer = columns // elem_size
    share_count = LANES // peer
    lane = lax.broadcasted_iota(jnp.int32, (8, LANES), 1)
    mine = lane // peer == lax.rem(me_elem, share_count)
    for k in range(elem_size):
        piece = routed[:, k // share_count * LANES : (k // share_count + 1) * LANES]
        shift = lax.rem(me_elem + (elem_size * share_count - k), share_count) * peer
        moved = jnp.where(mine, pltpu.roll(piece, shift, 1), 0.0)
        for q in range(group_size):
            flux_ref[k * group_size + q] = moved[q : q + 1]


def sum_kernel(*refs, group_size):
    heats = refs[:group_size]
    flux_ref, lw_ref, sw_ref, out_ref = refs[group_size:]
    total = heats[0][...]
    for ref in heats[1:]:
        total = total + ref[...]
    per = lw_ref.shape[0]
    lw_ref[...] = total[:per]
    sw_ref[...] = total[per:]
    blocks = out_ref.shape[1] // LANES
    count = flux_ref.shape[0] // blocks
    for b in range(blocks):
        piece = flux_ref[b * count : (b + 1) * count].reshape(count, LANES)
        out_ref[:, b * LANES : (b + 1) * LANES] = jnp.sum(piece, axis=0, keepdims=True)


def local(*args):
    layers, columns = args[0].shape
    lw, terms = args[11].shape
    sw = args[12].shape[0]
    group_size, elem_size = lax.axis_size("gpt"), lax.axis_size("elem")
    lw_rows, sw_rows, node_rows = up_to(lw, 16), up_to(sw, 16), up_to(terms // 2, 16)
    per = layers // group_size
    both = lw_rows + sw_rows
    vmem = pl.BlockSpec(memory_space=pltpu.VMEM)
    *heats, flux = pl.pallas_call(
        functools.partial(column_kernel, count=len(args), elem_size=elem_size, group_size=group_size),
        out_shape=[jax.ShapeDtypeStruct((2 * per, columns), F32)] * group_size
        + [jax.ShapeDtypeStruct((elem_size * group_size, 1, LANES), F32)],
        in_specs=[vmem] * len(args),
        out_specs=[vmem] * (group_size + 1),
        scratch_shapes=[
            pltpu.VMEM((both, 4 * node_rows), BF16),
            pltpu.VMEM((4 * per, 2 * per * both), BF16),
            pltpu.VMEM((layers, lw_rows, BLOCK), F32),
            pltpu.VMEM((layers, sw_rows, BLOCK), F32),
            pltpu.VMEM((2, group_size, per * both, BLOCK), BF16),
            pltpu.VMEM((group_size, 2 * per, columns), F32),
            pltpu.VMEM((5, layers, columns), F32),
            pltpu.VMEM((layers, columns), F32),
            pltpu.VMEM((layers, columns), F32),
            pltpu.VMEM((8, columns), F32),
            pltpu.VMEM((8, columns), F32),
        ],
        compiler_params=pltpu.CompilerParams(vmem_limit_bytes=24 << 20),
        name="columns",
    )(*[pltpu.with_memory_space_constraint(a, pltpu.HBM) for a in args])
    moved = [heats[0]]
    for d in range(1, group_size):
        moved.append(lax.ppermute(heats[d], "gpt", [(i, i ^ d) for i in range(group_size)]))
    flux = lax.all_to_all(flux, ("elem", "gpt"), 0, 0, tiled=True)
    return tuple(
        pl.pallas_call(
            functools.partial(sum_kernel, group_size=group_size),
            out_shape=[
                jax.ShapeDtypeStruct((per, columns), F32),
                jax.ShapeDtypeStruct((per, columns), F32),
                jax.ShapeDtypeStruct((1, columns), F32),
            ],
            in_specs=[vmem] * (group_size + 1),
            out_specs=[vmem] * 3,
            compiler_params=pltpu.CompilerParams(vmem_limit_bytes=2 << 20),
            name="sums",
        )(*moved, flux)
    )


def solution(mesh):
    in_specs = (P(None, "elem"),) * 6 + (P("elem"),) * 4 + (P(), P("gpt", None), P("gpt", None), P("gpt"), P("gpt"))
    out_specs = (P("gpt", "elem"), P("gpt", "elem"), P("gpt", "elem"))
    return jax.shard_map(local, mesh=mesh, in_specs=in_specs, out_specs=out_specs, check_vma=False)
```

```python
import functools

import jax
import jax.numpy as jnp
from jax import lax
from jax.experimental import pallas as pl
from jax.experimental.pallas import tpu as pltpu
from jax.sharding import PartitionSpec as P

F32 = jnp.float32
BF16 = jnp.bfloat16
LANES = 128
LOG2E = 1.4426950408889634
DIFFUSE = -1.66 * LOG2E


def up_to(count, step):
    return (count + step - 1) // step * step


def pick(row, index):
    blocks = row.shape[1] // LANES
    out = []
    for at in range(index.shape[1] // LANES):
        want = index[:, at * LANES : (at + 1) * LANES]
        inside = jnp.broadcast_to(want % LANES, (row.shape[0], LANES))
        got = None
        for b in range(blocks):
            piece = jnp.take_along_axis(row[:, b * LANES : (b + 1) * LANES], inside, axis=1, mode="promise_in_bounds")
            got = piece if b == 0 else jnp.where(want // LANES == b, piece, got)
        out.append(got)
    return jnp.concatenate(out, axis=1)


def column_of(row, rows, count):
    if count < rows:
        row = jnp.concatenate([row, jnp.zeros((1, rows - count), row.dtype)], axis=1)
    across = lax.broadcasted_iota(jnp.int32, (rows, rows), 1)
    down = lax.broadcasted_iota(jnp.int32, (rows, rows), 0)
    square = jnp.where(across == down, jnp.broadcast_to(row, (rows, rows)), 0.0)
    return jnp.sum(square, axis=1, keepdims=True)


def total(x, weights):
    x = x * weights
    out = x[:8]
    for r in range(8, x.shape[0], 8):
        out = out + x[r : r + 8]
    return jnp.sum(out, axis=0, keepdims=True)


def column_kernel(*refs, count, elem_size, group_size):
    ins, refs = refs[:count], refs[count:]
    kelvin_ref, moist_ref, diox_ref, depth_ref, slot_ref, share_ref, skin_ref, albedo_ref = ins[:8]
    sun_ref, routes_ref, angles_ref, thermal_ref, sunlight_ref, planck_ref, solar_ref = ins[8:]
    flux_ref, net_lw, net_sw, shares_ref, depth_out = refs[:5]
    table, passing, depths, downs, rows, warm, edge, sides, fluxes = refs[5:]
    layers, columns = kelvin_ref.shape
    lw, terms = thermal_ref.shape
    sw = sunlight_ref.shape[0]
    nodes = terms // 2
    lw_rows, sw_rows, node_rows = up_to(lw, 16), up_to(sw, 16), up_to(nodes, 16)
    both = lw_rows + sw_rows
    me_elem = lax.axis_index("elem")

    table[...] = jnp.zeros_like(table)
    for first, ref, size in ((0, thermal_ref, lw), (lw_rows, sunlight_ref, sw)):
        values = ref[...]
        for kind in range(2):
            here = values[:, kind * nodes : (kind + 1) * nodes]
            for pair in range(2):
                at = (2 * pair + kind) * node_rows
                table[pair * both + first : pair * both + first + size, at : at + nodes] = here

    planck_row = planck_ref[...].reshape(1, lw)
    solar_row = solar_ref[...].reshape(1, sw)
    pieces = [planck_row, jnp.zeros((1, lw_rows - lw), F32), solar_row, jnp.zeros((1, sw_rows - sw), F32)]
    shares_ref[...] = jnp.concatenate([p for p in pieces if p.shape[1]], axis=1)
    planck = column_of(planck_row, lw_rows, lw)
    solar = column_of(solar_row, sw_rows, sw)

    share = share_ref[...]
    rows[0] = slot_ref[...].astype(F32)
    rows[1] = (1.0 - share) * moist_ref[...]
    rows[2] = (1.0 - share) * diox_ref[...]
    rows[3] = share * moist_ref[...]
    rows[4] = share * diox_ref[...]
    relative = kelvin_ref[...] * (1.0 / 250.0)
    relative = relative * relative
    relative = relative * relative
    warm[...] = relative
    edge[0 : layers - 1] = relative[: layers - 1] - relative[1:]
    edge[layers - 1 : layers] = relative[layers - 1 :]

    angles = angles_ref[...].reshape(1, angles_ref.shape[0])
    bins = angles.shape[1]
    if bins % LANES:
        angles = jnp.concatenate([angles, jnp.zeros((1, up_to(bins, LANES) - bins), F32)], axis=1)
    sun = sun_ref[...].reshape(1, columns)
    angles = jnp.broadcast_to(angles, (8, angles.shape[1]))
    cosine = jnp.where(sun < bins, pick(angles, jnp.minimum(sun, angles.shape[1] - 1))[:1], 0.0)
    skin = skin_ref[...].reshape(1, columns) * (1.0 / 250.0)
    skin = skin * skin
    sides[0:1] = skin * skin
    sides[1:2] = albedo_ref[...].reshape(1, columns)
    sides[2:3] = (-LOG2E) / jnp.where(cosine > 0.0, cosine, 1.0)

    node_of_row = lax.broadcasted_iota(jnp.int32, (node_rows, columns), 0).astype(F32).astype(BF16)
    node_below = node_of_row - jnp.asarray(1.0, BF16)
    zero = jnp.zeros((node_rows, columns), BF16)

    def spread(kind, l):
        row = jnp.broadcast_to(rows[kind, l : l + 1, :], (16, columns)).astype(BF16)
        return jnp.concatenate([row] * (node_rows // 16), axis=0)

    slant = sides[2:3, :]
    down = jnp.broadcast_to(-warm[0:1, :], (lw_rows, columns))
    beam = jnp.ones((sw_rows, columns), F32)
    net_sw[0] = beam
    for l in range(layers):
        if l % 2 == 0:
            amounts = []
            for at in (l, l + 1):
                node = spread(0, at)
                lower, upper = node_of_row == node, node_below == node
                for kind in (1, 2):
                    rest = jnp.where(upper, spread(kind + 2, at), zero)
                    amounts.append(jnp.where(lower, spread(kind, at), rest))
            pair = jnp.dot(table[...], jnp.concatenate(amounts, axis=0), preferred_element_type=F32)
        tau = pair[l % 2 * both : (l % 2 + 1) * both]
        through = jnp.exp2(DIFFUSE * tau[:lw_rows])
        passed = through * down
        passing[l] = through
        downs[l] = down
        down = passed + edge[l : l + 1]
        tau = tau[lw_rows:]
        depths[l] = tau
        beam = beam * jnp.exp2(slant * tau)
        net_sw[l + 1] = beam
    up = jnp.broadcast_to(sides[0:1, :], (lw_rows, columns))
    net_lw[layers] = up - down
    up = up - warm[layers - 1 : layers, :]
    back = sides[1:2, :] * beam
    fluxes[0:1, :] = total(down, planck)
    fluxes[2:3, :] = total(beam, solar)
    net_sw[layers] = beam - back
    for l in reversed(range(layers)):
        passed = passing[l] * up
        net_lw[l] = passed - downs[l]
        up = passed - edge[l - 1 : l, :] if l else passed + warm[0:1, :]
        back = back * jnp.exp2(DIFFUSE * depths[l])
        net_sw[l] = net_sw[l] - back
    fluxes[1:2, :] = total(up, planck)
    fluxes[3:4, :] = total(back, solar)


    depth_out[0:layers] = depth_ref[...]
    depth_out[layers : layers + 8] = jnp.broadcast_to(cosine, (8, columns))
    row = lax.broadcasted_iota(jnp.int32, (8, columns), 0)
    routed = pick(fluxes[...] * jnp.where(row < 2, 1.0, cosine), routes_ref[...].reshape(1, columns))
    peer = columns // elem_size
    share_count = LANES // peer
    lane = lax.broadcasted_iota(jnp.int32, (8, LANES), 1)
    mine = lane // peer == lax.rem(me_elem, share_count)
    for k in range(elem_size):
        piece = routed[:, k // share_count * LANES : (k // share_count + 1) * LANES]
        shift = lax.rem(me_elem + (elem_size * share_count - k), share_count) * peer
        moved = jnp.where(mine, pltpu.roll(piece, shift, 1), 0.0)
        for q in range(group_size):
            flux_ref[k * group_size + q] = moved[q : q + 1]


def heat_kernel(net_lw, net_sw, shares_ref, depth_ref, *heat_refs_and_heat):
    heat_refs, heat = heat_refs_and_heat[:-1], heat_refs_and_heat[-1]
    group_size = len(heat_refs)
    faces, lw_rows, columns = net_lw.shape
    layers = faces - 1
    both = shares_ref.shape[1]
    per = layers // group_size
    me_gpt = lax.axis_index("gpt")
    shares = jnp.broadcast_to(jnp.concatenate([shares_ref[...]] * per, axis=1), (2 * per, per * both))
    lane = lax.broadcasted_iota(jnp.int32, shares.shape, 1)
    wanted = lax.div(lane, both) + jnp.where(lax.rem(lane, both) < lw_rows, 0, per)
    shares = jnp.where(lax.broadcasted_iota(jnp.int32, shares.shape, 0) == wanted, shares, 0.0)
    high = shares.astype(BF16).astype(F32)
    weights = jnp.concatenate([high, shares - high], axis=0).astype(BF16)
    inverse = 1.0 / depth_ref[0:layers]
    cosine = depth_ref[layers : layers + 1]
    for q in range(group_size):
        gains = []
        for l in range(q * per, (q + 1) * per):
            gains.append((net_lw[l + 1] - net_lw[l]).astype(BF16))
            gains.append((net_sw[l] - net_sw[l + 1]).astype(BF16))
        sums = jnp.dot(weights, jnp.concatenate(gains, axis=0), preferred_element_type=F32)
        scale = inverse[q * per : (q + 1) * per]
        scale = jnp.concatenate([scale, scale * cosine], axis=0)
        heat[q] = (sums[: 2 * per] + sums[2 * per :]) * scale
    for d in range(group_size):
        heat_refs[d][...] = heat[jnp.bitwise_xor(me_gpt, d)]


def sum_kernel(*refs, group_size):
    heats = refs[:group_size]
    flux_ref, lw_ref, sw_ref, out_ref = refs[group_size:]
    total = heats[0][...]
    for ref in heats[1:]:
        total = total + ref[...]
    per = lw_ref.shape[0]
    lw_ref[...] = total[:per]
    sw_ref[...] = total[per:]
    blocks = out_ref.shape[1] // LANES
    count = flux_ref.shape[0] // blocks
    for b in range(blocks):
        piece = flux_ref[b * count : (b + 1) * count].reshape(count, LANES)
        out_ref[:, b * LANES : (b + 1) * LANES] = jnp.sum(piece, axis=0, keepdims=True)


def local(*args):
    layers, columns = args[0].shape
    lw, terms = args[11].shape
    sw = args[12].shape[0]
    group_size, elem_size = lax.axis_size("gpt"), lax.axis_size("elem")
    lw_rows, sw_rows, node_rows = up_to(lw, 16), up_to(sw, 16), up_to(terms // 2, 16)
    per = layers // group_size
    both = lw_rows + sw_rows
    vmem = pl.BlockSpec(memory_space=pltpu.VMEM)

    def out(*shape):
        return jax.ShapeDtypeStruct(shape, F32)

    flux, *states = pl.pallas_call(
        functools.partial(column_kernel, count=len(args), elem_size=elem_size, group_size=group_size),
        out_shape=[
            out(elem_size * group_size, 1, LANES),
            out(layers + 1, lw_rows, columns),
            out(layers + 1, sw_rows, columns),
            out(1, both),
            out(layers + 8, columns),
        ],
        in_specs=[vmem] * len(args),
        out_specs=[vmem] * 5,
        scratch_shapes=[
            pltpu.VMEM((2 * both, 4 * node_rows), BF16),
            pltpu.VMEM((layers, lw_rows, columns), F32),
            pltpu.VMEM((layers, sw_rows, columns), F32),
            pltpu.VMEM((layers, lw_rows, columns), F32),
            pltpu.VMEM((5, layers, columns), F32),
            pltpu.VMEM((layers, columns), F32),
            pltpu.VMEM((layers, columns), F32),
            pltpu.VMEM((8, columns), F32),
            pltpu.VMEM((8, columns), F32),
        ],
        compiler_params=pltpu.CompilerParams(vmem_limit_bytes=24 << 20),
        name="columns",
    )(*[pltpu.with_memory_space_constraint(a, pltpu.HBM) for a in args])
    heats = pl.pallas_call(
        heat_kernel,
        out_shape=[out(2 * per, columns)] * group_size,
        in_specs=[vmem] * len(states),
        out_specs=[vmem] * group_size,
        scratch_shapes=[pltpu.VMEM((group_size, 2 * per, columns), F32)],
        compiler_params=pltpu.CompilerParams(vmem_limit_bytes=8 << 20),
        name="heat",
    )(*states)
    moved = [heats[0]]
    for d in range(1, group_size):
        moved.append(lax.ppermute(heats[d], "gpt", [(i, i ^ d) for i in range(group_size)]))
    flux = lax.all_to_all(flux, ("elem", "gpt"), 0, 0, tiled=True)
    return tuple(
        pl.pallas_call(
            functools.partial(sum_kernel, group_size=group_size),
            out_shape=[
                jax.ShapeDtypeStruct((per, columns), F32),
                jax.ShapeDtypeStruct((per, columns), F32),
                jax.ShapeDtypeStruct((1, columns), F32),
            ],
            in_specs=[vmem] * (group_size + 1),
            out_specs=[vmem] * 3,
            compiler_params=pltpu.CompilerParams(vmem_limit_bytes=2 << 20),
            name="sums",
        )(*moved, flux)
    )


def solution(mesh):
    in_specs = (P(None, "elem"),) * 6 + (P("elem"),) * 4 + (P(), P("gpt", None), P("gpt", None), P("gpt"), P("gpt"))
    out_specs = (P("gpt", "elem"), P("gpt", "elem"), P("gpt", "elem"))
    return jax.shard_map(local, mesh=mesh, in_specs=in_specs, out_specs=out_specs, check_vma=False)
```

```python
import functools

import jax
import jax.numpy as jnp
from jax import lax
from jax.experimental import pallas as pl
from jax.experimental.pallas import tpu as pltpu
from jax.sharding import PartitionSpec as P

F32 = jnp.float32
BF16 = jnp.bfloat16
LANES = 128
LOG2E = 1.4426950408889634
DIFFUSE = -1.66 * LOG2E


def up_to(count, step):
    return (count + step - 1) // step * step


def pick(row, index):
    blocks = row.shape[1] // LANES
    out = []
    for at in range(index.shape[1] // LANES):
        want = index[:, at * LANES : (at + 1) * LANES]
        inside = jnp.broadcast_to(want % LANES, (row.shape[0], LANES))
        got = None
        for b in range(blocks):
            piece = jnp.take_along_axis(row[:, b * LANES : (b + 1) * LANES], inside, axis=1, mode="promise_in_bounds")
            got = piece if b == 0 else jnp.where(want // LANES == b, piece, got)
        out.append(got)
    return jnp.concatenate(out, axis=1)


def column_of(row, rows, count):
    if count < rows:
        row = jnp.concatenate([row, jnp.zeros((1, rows - count), row.dtype)], axis=1)
    across = lax.broadcasted_iota(jnp.int32, (rows, rows), 1)
    down = lax.broadcasted_iota(jnp.int32, (rows, rows), 0)
    square = jnp.where(across == down, jnp.broadcast_to(row, (rows, rows)), 0.0)
    return jnp.sum(square, axis=1, keepdims=True)


def total(x, weights):
    x = x * weights
    out = x[:8]
    for r in range(8, x.shape[0], 8):
        out = out + x[r : r + 8]
    return jnp.sum(out, axis=0, keepdims=True)


def column_kernel(*refs, count, elem_size, group_size):
    ins, refs = refs[:count], refs[count:]
    kelvin_ref, moist_ref, diox_ref, depth_ref, slot_ref, share_ref, skin_ref, albedo_ref = ins[:8]
    sun_ref, routes_ref, angles_ref, thermal_ref, sunlight_ref, planck_ref, solar_ref = ins[8:]
    flux_ref, net_lw, depths, shares_ref, depth_out = refs[:5]
    table, passing, downs, rows, warm, edge, sides, fluxes = refs[5:]
    layers, columns = kelvin_ref.shape
    lw, terms = thermal_ref.shape
    sw = sunlight_ref.shape[0]
    nodes = terms // 2
    lw_rows, sw_rows, node_rows = up_to(lw, 16), up_to(sw, 16), up_to(nodes, 16)
    both = lw_rows + sw_rows
    me_elem = lax.axis_index("elem")

    table[...] = jnp.zeros_like(table)
    for first, ref, size in ((0, thermal_ref, lw), (lw_rows, sunlight_ref, sw)):
        values = ref[...]
        for kind in range(2):
            here = values[:, kind * nodes : (kind + 1) * nodes]
            for pair in range(2):
                at = (2 * pair + kind) * node_rows
                table[pair * both + first : pair * both + first + size, at : at + nodes] = here

    planck_row = planck_ref[...].reshape(1, lw)
    solar_row = solar_ref[...].reshape(1, sw)
    pieces = [planck_row, jnp.zeros((1, lw_rows - lw), F32), solar_row, jnp.zeros((1, sw_rows - sw), F32)]
    shares_ref[...] = jnp.concatenate([p for p in pieces if p.shape[1]], axis=1)
    planck = column_of(planck_row, lw_rows, lw)
    solar = column_of(solar_row, sw_rows, sw)

    share = share_ref[...]
    rows[0] = slot_ref[...].astype(F32)
    rows[1] = (1.0 - share) * moist_ref[...]
    rows[2] = (1.0 - share) * diox_ref[...]
    rows[3] = share * moist_ref[...]
    rows[4] = share * diox_ref[...]
    relative = kelvin_ref[...] * (1.0 / 250.0)
    relative = relative * relative
    relative = relative * relative
    warm[...] = relative
    edge[0 : layers - 1] = relative[: layers - 1] - relative[1:]
    edge[layers - 1 : layers] = relative[layers - 1 :]

    angles = angles_ref[...].reshape(1, angles_ref.shape[0])
    bins = angles.shape[1]
    if bins % LANES:
        angles = jnp.concatenate([angles, jnp.zeros((1, up_to(bins, LANES) - bins), F32)], axis=1)
    sun = sun_ref[...].reshape(1, columns)
    angles = jnp.broadcast_to(angles, (8, angles.shape[1]))
    cosine = jnp.where(sun < bins, pick(angles, jnp.minimum(sun, angles.shape[1] - 1))[:1], 0.0)
    skin = skin_ref[...].reshape(1, columns) * (1.0 / 250.0)
    skin = skin * skin
    sides[0:1] = skin * skin
    albedo = albedo_ref[...].reshape(1, columns)
    slant = (-LOG2E) / jnp.where(cosine > 0.0, cosine, 1.0)
    for i, side in enumerate((cosine, slant, albedo)):
        depth_out[layers + i : layers + i + 1] = side

    node_of_row = lax.broadcasted_iota(jnp.int32, (node_rows, columns), 0).astype(F32).astype(BF16)
    node_below = node_of_row - jnp.asarray(1.0, BF16)
    zero = jnp.zeros((node_rows, columns), BF16)

    def spread(kind, l):
        row = jnp.broadcast_to(rows[kind, l : l + 1, :], (16, columns)).astype(BF16)
        return jnp.concatenate([row] * (node_rows // 16), axis=0)

    down = jnp.broadcast_to(-warm[0:1, :], (lw_rows, columns))
    depth = jnp.zeros((sw_rows, columns), F32)
    for l in range(layers):
        if l % 2 == 0:
            amounts = []
            for at in (l, l + 1):
                node = spread(0, at)
                lower, upper = node_of_row == node, node_below == node
                for kind in (1, 2):
                    rest = jnp.where(upper, spread(kind + 2, at), zero)
                    amounts.append(jnp.where(lower, spread(kind, at), rest))
            pair = jnp.dot(table[...], jnp.concatenate(amounts, axis=0), preferred_element_type=F32)
        tau = pair[l % 2 * both : (l % 2 + 1) * both]
        through = jnp.exp2(DIFFUSE * tau[:lw_rows])
        passed = through * down
        passing[l] = through
        downs[l] = down
        down = passed + edge[l : l + 1]
        tau = tau[lw_rows:]
        depths[l] = tau
        depth = depth + tau
    up = jnp.broadcast_to(sides[0:1, :], (lw_rows, columns))
    net_lw[layers] = up - down
    up = up - warm[layers - 1 : layers, :]
    beam = jnp.exp2(slant * depth)
    fluxes[0:1, :] = total(down, planck)
    fluxes[2:3, :] = total(beam, solar)
    fluxes[3:4, :] = total(albedo * beam * jnp.exp2(DIFFUSE * depth), solar)
    for l in reversed(range(layers)):
        passed = passing[l] * up
        net_lw[l] = passed - downs[l]
        up = passed - edge[l - 1 : l, :] if l else passed + warm[0:1, :]
    fluxes[1:2, :] = total(up, planck)


    depth_out[0:layers] = depth_ref[...]
    row = lax.broadcasted_iota(jnp.int32, (8, columns), 0)
    routed = pick(fluxes[...] * jnp.where(row < 2, 1.0, cosine), routes_ref[...].reshape(1, columns))
    peer = columns // elem_size
    share_count = LANES // peer
    lane = lax.broadcasted_iota(jnp.int32, (8, LANES), 1)
    mine = lane // peer == lax.rem(me_elem, share_count)
    for k in range(elem_size):
        piece = routed[:, k // share_count * LANES : (k // share_count + 1) * LANES]
        shift = lax.rem(me_elem + (elem_size * share_count - k), share_count) * peer
        moved = jnp.where(mine, pltpu.roll(piece, shift, 1), 0.0)
        for q in range(group_size):
            flux_ref[k * group_size + q] = moved[q : q + 1]


def heat_kernel(net_lw, depths, shares_ref, depth_ref, *rest):
    heat_refs, heat, falls = rest[:-2], rest[-2], rest[-1]
    group_size = len(heat_refs)
    faces, lw_rows, columns = net_lw.shape
    layers = faces - 1
    both = shares_ref.shape[1]
    per = layers // group_size
    me_gpt = lax.axis_index("gpt")
    shares = jnp.broadcast_to(jnp.concatenate([shares_ref[...]] * per, axis=1), (2 * per, per * both))
    lane = lax.broadcasted_iota(jnp.int32, shares.shape, 1)
    wanted = lax.div(lane, both) + jnp.where(lax.rem(lane, both) < lw_rows, 0, per)
    shares = jnp.where(lax.broadcasted_iota(jnp.int32, shares.shape, 0) == wanted, shares, 0.0)
    high = shares.astype(BF16).astype(F32)
    weights = jnp.concatenate([high, shares - high], axis=0).astype(BF16)
    inverse = 1.0 / depth_ref[0:layers]
    cosine, slant, albedo = (depth_ref[layers + i : layers + i + 1] for i in range(3))
    beam = jnp.ones(depths.shape[1:], F32)
    for l in range(layers):
        passed = beam * jnp.exp2(slant * depths[l])
        falls[l] = beam - passed
        beam = passed
    back = albedo * beam
    for q in reversed(range(group_size)):
        gains = []
        for l in reversed(range(q * per, (q + 1) * per)):
            passed = back * jnp.exp2(DIFFUSE * depths[l])
            gains.append(((back - passed) + falls[l]).astype(BF16))
            gains.append((net_lw[l + 1] - net_lw[l]).astype(BF16))
            back = passed
        gains.reverse()
        sums = jnp.dot(weights, jnp.concatenate(gains, axis=0), preferred_element_type=F32)
        scale = inverse[q * per : (q + 1) * per]
        scale = jnp.concatenate([scale, scale * cosine], axis=0)
        heat[q] = (sums[: 2 * per] + sums[2 * per :]) * scale
    for d in range(group_size):
        heat_refs[d][...] = heat[jnp.bitwise_xor(me_gpt, d)]


def sum_kernel(*refs, group_size):
    heats = refs[:group_size]
    flux_ref, lw_ref, sw_ref, out_ref = refs[group_size:]
    total = heats[0][...]
    for ref in heats[1:]:
        total = total + ref[...]
    per = lw_ref.shape[0]
    lw_ref[...] = total[:per]
    sw_ref[...] = total[per:]
    blocks = out_ref.shape[1] // LANES
    count = flux_ref.shape[0] // blocks
    for b in range(blocks):
        piece = flux_ref[b * count : (b + 1) * count].reshape(count, LANES)
        out_ref[:, b * LANES : (b + 1) * LANES] = jnp.sum(piece, axis=0, keepdims=True)


def local(*args):
    layers, columns = args[0].shape
    lw, terms = args[11].shape
    sw = args[12].shape[0]
    group_size, elem_size = lax.axis_size("gpt"), lax.axis_size("elem")
    lw_rows, sw_rows, node_rows = up_to(lw, 16), up_to(sw, 16), up_to(terms // 2, 16)
    per = layers // group_size
    both = lw_rows + sw_rows
    vmem = pl.BlockSpec(memory_space=pltpu.VMEM)

    def out(*shape):
        return jax.ShapeDtypeStruct(shape, F32)

    flux, *states = pl.pallas_call(
        functools.partial(column_kernel, count=len(args), elem_size=elem_size, group_size=group_size),
        out_shape=[
            out(elem_size * group_size, 1, LANES),
            out(layers + 1, lw_rows, columns),
            out(layers, sw_rows, columns),
            out(1, both),
            out(layers + 8, columns),
        ],
        in_specs=[vmem] * len(args),
        out_specs=[vmem] * 5,
        scratch_shapes=[
            pltpu.VMEM((2 * both, 4 * node_rows), BF16),
            pltpu.VMEM((layers, lw_rows, columns), F32),
            pltpu.VMEM((layers, lw_rows, columns), F32),
            pltpu.VMEM((5, layers, columns), F32),
            pltpu.VMEM((layers, columns), F32),
            pltpu.VMEM((layers, columns), F32),
            pltpu.VMEM((8, columns), F32),
            pltpu.VMEM((8, columns), F32),
        ],
        compiler_params=pltpu.CompilerParams(vmem_limit_bytes=24 << 20),
        name="columns",
    )(*[pltpu.with_memory_space_constraint(a, pltpu.HBM) for a in args])
    heats = pl.pallas_call(
        heat_kernel,
        out_shape=[out(2 * per, columns)] * group_size,
        in_specs=[vmem] * len(states),
        out_specs=[vmem] * group_size,
        scratch_shapes=[
            pltpu.VMEM((group_size, 2 * per, columns), F32),
            pltpu.VMEM((layers, sw_rows, columns), F32),
        ],
        compiler_params=pltpu.CompilerParams(vmem_limit_bytes=8 << 20),
        name="heat",
    )(*states)
    moved = [heats[0]]
    for d in range(1, group_size):
        moved.append(lax.ppermute(heats[d], "gpt", [(i, i ^ d) for i in range(group_size)]))
    flux = lax.all_to_all(flux, ("elem", "gpt"), 0, 0, tiled=True)
    return tuple(
        pl.pallas_call(
            functools.partial(sum_kernel, group_size=group_size),
            out_shape=[
                jax.ShapeDtypeStruct((per, columns), F32),
                jax.ShapeDtypeStruct((per, columns), F32),
                jax.ShapeDtypeStruct((1, columns), F32),
            ],
            in_specs=[vmem] * (group_size + 1),
            out_specs=[vmem] * 3,
            compiler_params=pltpu.CompilerParams(vmem_limit_bytes=2 << 20),
            name="sums",
        )(*moved, flux)
    )


def solution(mesh):
    in_specs = (P(None, "elem"),) * 6 + (P("elem"),) * 4 + (P(), P("gpt", None), P("gpt", None), P("gpt"), P("gpt"))
    out_specs = (P("gpt", "elem"), P("gpt", "elem"), P("gpt", "elem"))
    return jax.shard_map(local, mesh=mesh, in_specs=in_specs, out_specs=out_specs, check_vma=False)
```

```python
import functools

import jax
import jax.numpy as jnp
from jax import lax
from jax.experimental import pallas as pl
from jax.experimental.pallas import tpu as pltpu
from jax.sharding import PartitionSpec as P

F32 = jnp.float32
BF16 = jnp.bfloat16
LANES = 128
LOG2E = 1.4426950408889634
DIFFUSE = -1.66 * LOG2E


def up_to(count, step):
    return (count + step - 1) // step * step


def pick(row, index):
    blocks = row.shape[1] // LANES
    out = []
    for at in range(index.shape[1] // LANES):
        want = index[:, at * LANES : (at + 1) * LANES]
        inside = jnp.broadcast_to(want % LANES, (row.shape[0], LANES))
        got = None
        for b in range(blocks):
            piece = jnp.take_along_axis(row[:, b * LANES : (b + 1) * LANES], inside, axis=1, mode="promise_in_bounds")
            got = piece if b == 0 else jnp.where(want // LANES == b, piece, got)
        out.append(got)
    return jnp.concatenate(out, axis=1)


def column_of(row, rows, count):
    if count < rows:
        row = jnp.concatenate([row, jnp.zeros((1, rows - count), row.dtype)], axis=1)
    across = lax.broadcasted_iota(jnp.int32, (rows, rows), 1)
    down = lax.broadcasted_iota(jnp.int32, (rows, rows), 0)
    square = jnp.where(across == down, jnp.broadcast_to(row, (rows, rows)), 0.0)
    return jnp.sum(square, axis=1, keepdims=True)


def total(x, weights):
    x = x * weights
    out = x[:8]
    for r in range(8, x.shape[0], 8):
        out = out + x[r : r + 8]
    return jnp.sum(out, axis=0, keepdims=True)


def column_kernel(*refs, count, elem_size, group_size):
    ins, refs = refs[:count], refs[count:]
    kelvin_ref, moist_ref, diox_ref, depth_ref, slot_ref, share_ref, skin_ref, albedo_ref = ins[:8]
    sun_ref, routes_ref, angles_ref, thermal_ref, sunlight_ref, planck_ref, solar_ref = ins[8:]
    flux_ref, downs, ups, depths, shares_ref, depth_out = refs[:6]
    table, passing, rows, warm, edge, sides, fluxes = refs[6:]
    layers, columns = kelvin_ref.shape
    lw, terms = thermal_ref.shape
    sw = sunlight_ref.shape[0]
    nodes = terms // 2
    lw_rows, sw_rows, node_rows = up_to(lw, 16), up_to(sw, 16), up_to(nodes, 16)
    both = lw_rows + sw_rows
    me_elem = lax.axis_index("elem")

    table[...] = jnp.zeros_like(table)
    for first, ref, size in ((0, thermal_ref, lw), (lw_rows, sunlight_ref, sw)):
        values = ref[...]
        for kind in range(2):
            here = values[:, kind * nodes : (kind + 1) * nodes]
            for pair in range(2):
                at = (2 * pair + kind) * node_rows
                table[pair * both + first : pair * both + first + size, at : at + nodes] = here

    planck_row = planck_ref[...].reshape(1, lw)
    solar_row = solar_ref[...].reshape(1, sw)
    pieces = [planck_row, jnp.zeros((1, lw_rows - lw), F32), solar_row, jnp.zeros((1, sw_rows - sw), F32)]
    shares_ref[...] = jnp.concatenate([p for p in pieces if p.shape[1]], axis=1)
    planck = column_of(planck_row, lw_rows, lw)
    solar = column_of(solar_row, sw_rows, sw)

    share = share_ref[...]
    rows[0] = slot_ref[...].astype(F32)
    rows[1] = (1.0 - share) * moist_ref[...]
    rows[2] = (1.0 - share) * diox_ref[...]
    rows[3] = share * moist_ref[...]
    rows[4] = share * diox_ref[...]
    relative = kelvin_ref[...] * (1.0 / 250.0)
    relative = relative * relative
    relative = relative * relative
    warm[...] = relative
    edge[0 : layers - 1] = relative[: layers - 1] - relative[1:]
    edge[layers - 1 : layers] = relative[layers - 1 :]

    angles = angles_ref[...].reshape(1, angles_ref.shape[0])
    bins = angles.shape[1]
    if bins % LANES:
        angles = jnp.concatenate([angles, jnp.zeros((1, up_to(bins, LANES) - bins), F32)], axis=1)
    sun = sun_ref[...].reshape(1, columns)
    angles = jnp.broadcast_to(angles, (8, angles.shape[1]))
    cosine = jnp.where(sun < bins, pick(angles, jnp.minimum(sun, angles.shape[1] - 1))[:1], 0.0)
    skin = skin_ref[...].reshape(1, columns) * (1.0 / 250.0)
    skin = skin * skin
    sides[0:1] = skin * skin
    albedo = albedo_ref[...].reshape(1, columns)
    slant = (-LOG2E) / jnp.where(cosine > 0.0, cosine, 1.0)
    for i, side in enumerate((cosine, slant, albedo)):
        depth_out[layers + i : layers + i + 1] = side

    node_of_row = lax.broadcasted_iota(jnp.int32, (node_rows, columns), 0).astype(F32).astype(BF16)
    node_below = node_of_row - jnp.asarray(1.0, BF16)
    zero = jnp.zeros((node_rows, columns), BF16)

    def spread(kind, l):
        row = jnp.broadcast_to(rows[kind, l : l + 1, :], (16, columns)).astype(BF16)
        return jnp.concatenate([row] * (node_rows // 16), axis=0)

    down = jnp.broadcast_to(-warm[0:1, :], (lw_rows, columns))
    depth = jnp.zeros((sw_rows, columns), F32)
    for l in range(layers):
        if l % 2 == 0:
            amounts = []
            for at in (l, l + 1):
                node = spread(0, at)
                lower, upper = node_of_row == node, node_below == node
                for kind in (1, 2):
                    rest = jnp.where(upper, spread(kind + 2, at), zero)
                    amounts.append(jnp.where(lower, spread(kind, at), rest))
            pair = jnp.dot(table[...], jnp.concatenate(amounts, axis=0), preferred_element_type=F32)
        tau = pair[l % 2 * both : (l % 2 + 1) * both]
        through = jnp.exp2(DIFFUSE * tau[:lw_rows])
        passed = through * down
        passing[l] = through
        downs[l] = down
        down = passed + edge[l : l + 1]
        tau = tau[lw_rows:]
        depths[l] = tau
        depth = depth + tau
    up = jnp.broadcast_to(sides[0:1, :], (lw_rows, columns))
    ups[layers] = up - down
    up = up - warm[layers - 1 : layers, :]
    beam = jnp.exp2(slant * depth)
    fluxes[0:1, :] = total(down, planck)
    fluxes[2:3, :] = total(beam, solar)
    fluxes[3:4, :] = total(albedo * beam * jnp.exp2(DIFFUSE * depth), solar)
    for l in reversed(range(layers)):
        passed = passing[l] * up
        ups[l] = passed
        up = passed - edge[l - 1 : l, :] if l else passed + warm[0:1, :]
    fluxes[1:2, :] = total(up, planck)

    depth_out[0:layers] = depth_ref[...]
    row = lax.broadcasted_iota(jnp.int32, (8, columns), 0)
    routed = pick(fluxes[...] * jnp.where(row < 2, 1.0, cosine), routes_ref[...].reshape(1, columns))
    peer = columns // elem_size
    share_count = LANES // peer
    lane = lax.broadcasted_iota(jnp.int32, (8, LANES), 1)
    mine = lane // peer == lax.rem(me_elem, share_count)
    for k in range(elem_size):
        piece = routed[:, k // share_count * LANES : (k // share_count + 1) * LANES]
        shift = lax.rem(me_elem + (elem_size * share_count - k), share_count) * peer
        moved = jnp.where(mine, pltpu.roll(piece, shift, 1), 0.0)
        for q in range(group_size):
            flux_ref[k * group_size + q] = moved[q : q + 1]


def heat_kernel(downs, ups, depths, shares_ref, depth_ref, *rest):
    heat_refs, heat, falls = rest[:-2], rest[-2], rest[-1]
    group_size = len(heat_refs)
    layers, lw_rows, columns = downs.shape
    both = shares_ref.shape[1]
    per = layers // group_size
    me_gpt = lax.axis_index("gpt")
    shares = jnp.broadcast_to(jnp.concatenate([shares_ref[...]] * per, axis=1), (2 * per, per * both))
    lane = lax.broadcasted_iota(jnp.int32, shares.shape, 1)
    wanted = lax.div(lane, both) + jnp.where(lax.rem(lane, both) < lw_rows, 0, per)
    shares = jnp.where(lax.broadcasted_iota(jnp.int32, shares.shape, 0) == wanted, shares, 0.0)
    high = shares.astype(BF16).astype(F32)
    weights = jnp.concatenate([high, shares - high], axis=0).astype(BF16)
    inverse = 1.0 / depth_ref[0:layers]
    cosine, slant, albedo = (depth_ref[layers + i : layers + i + 1] for i in range(3))
    beam = jnp.ones(depths.shape[1:], F32)
    for l in range(layers):
        passed = beam * jnp.exp2(slant * depths[l])
        falls[l] = beam - passed
        beam = passed
    back = albedo * beam
    net = ups[layers]
    for q in reversed(range(group_size)):
        gains = []
        for l in reversed(range(q * per, (q + 1) * per)):
            passed = back * jnp.exp2(DIFFUSE * depths[l])
            gains.append(((back - passed) + falls[l]).astype(BF16))
            face = ups[l] - downs[l]
            gains.append((net - face).astype(BF16))
            back, net = passed, face
        gains.reverse()
        sums = jnp.dot(weights, jnp.concatenate(gains, axis=0), preferred_element_type=F32)
        scale = inverse[q * per : (q + 1) * per]
        scale = jnp.concatenate([scale, scale * cosine], axis=0)
        heat[q] = (sums[: 2 * per] + sums[2 * per :]) * scale
    for d in range(group_size):
        heat_refs[d][...] = heat[jnp.bitwise_xor(me_gpt, d)]


def sum_kernel(*refs, group_size):
    heats = refs[:group_size]
    flux_ref, lw_ref, sw_ref, out_ref = refs[group_size:]
    total = heats[0][...]
    for ref in heats[1:]:
        total = total + ref[...]
    per = lw_ref.shape[0]
    lw_ref[...] = total[:per]
    sw_ref[...] = total[per:]
    blocks = out_ref.shape[1] // LANES
    count = flux_ref.shape[0] // blocks
    for b in range(blocks):
        piece = flux_ref[b * count : (b + 1) * count].reshape(count, LANES)
        out_ref[:, b * LANES : (b + 1) * LANES] = jnp.sum(piece, axis=0, keepdims=True)


def local(*args):
    layers, columns = args[0].shape
    lw, terms = args[11].shape
    sw = args[12].shape[0]
    group_size, elem_size = lax.axis_size("gpt"), lax.axis_size("elem")
    lw_rows, sw_rows, node_rows = up_to(lw, 16), up_to(sw, 16), up_to(terms // 2, 16)
    per = layers // group_size
    both = lw_rows + sw_rows
    vmem = pl.BlockSpec(memory_space=pltpu.VMEM)

    def out(*shape):
        return jax.ShapeDtypeStruct(shape, F32)

    flux, *states = pl.pallas_call(
        functools.partial(column_kernel, count=len(args), elem_size=elem_size, group_size=group_size),
        out_shape=[
            out(elem_size * group_size, 1, LANES),
            out(layers, lw_rows, columns),
            out(layers + 1, lw_rows, columns),
            out(layers, sw_rows, columns),
            out(1, both),
            out(layers + 8, columns),
        ],
        in_specs=[vmem] * len(args),
        out_specs=[vmem] * 6,
        scratch_shapes=[
            pltpu.VMEM((2 * both, 4 * node_rows), BF16),
            pltpu.VMEM((layers, lw_rows, columns), F32),
            pltpu.VMEM((5, layers, columns), F32),
            pltpu.VMEM((layers, columns), F32),
            pltpu.VMEM((layers, columns), F32),
            pltpu.VMEM((8, columns), F32),
            pltpu.VMEM((8, columns), F32),
        ],
        compiler_params=pltpu.CompilerParams(vmem_limit_bytes=24 << 20),
        name="columns",
    )(*[pltpu.with_memory_space_constraint(a, pltpu.HBM) for a in args])
    heats = pl.pallas_call(
        heat_kernel,
        out_shape=[out(2 * per, columns)] * group_size,
        in_specs=[vmem] * len(states),
        out_specs=[vmem] * group_size,
        scratch_shapes=[
            pltpu.VMEM((group_size, 2 * per, columns), F32),
            pltpu.VMEM((layers, sw_rows, columns), F32),
        ],
        compiler_params=pltpu.CompilerParams(vmem_limit_bytes=8 << 20),
        name="heat",
    )(*states)
    moved = [heats[0]]
    for d in range(1, group_size):
        moved.append(lax.ppermute(heats[d], "gpt", [(i, i ^ d) for i in range(group_size)]))
    flux = lax.all_to_all(flux, ("elem", "gpt"), 0, 0, tiled=True)
    return tuple(
        pl.pallas_call(
            functools.partial(sum_kernel, group_size=group_size),
            out_shape=[
                jax.ShapeDtypeStruct((per, columns), F32),
                jax.ShapeDtypeStruct((per, columns), F32),
                jax.ShapeDtypeStruct((1, columns), F32),
            ],
            in_specs=[vmem] * (group_size + 1),
            out_specs=[vmem] * 3,
            compiler_params=pltpu.CompilerParams(vmem_limit_bytes=2 << 20),
            name="sums",
        )(*moved, flux)
    )


def solution(mesh):
    in_specs = (P(None, "elem"),) * 6 + (P("elem"),) * 4 + (P(), P("gpt", None), P("gpt", None), P("gpt"), P("gpt"))
    out_specs = (P("gpt", "elem"), P("gpt", "elem"), P("gpt", "elem"))
    return jax.shard_map(local, mesh=mesh, in_specs=in_specs, out_specs=out_specs, check_vma=False)
```

```python
import functools

import jax
import jax.numpy as jnp
from jax import lax
from jax.experimental import pallas as pl
from jax.experimental.pallas import tpu as pltpu
from jax.sharding import PartitionSpec as P

F32 = jnp.float32
BF16 = jnp.bfloat16
LANES = 128
LOG2E = 1.4426950408889634
DIFFUSE = -1.66 * LOG2E


def up_to(count, step):
    return (count + step - 1) // step * step


def pick(row, index):
    blocks = row.shape[1] // LANES
    out = []
    for at in range(index.shape[1] // LANES):
        want = index[:, at * LANES : (at + 1) * LANES]
        inside = jnp.broadcast_to(want % LANES, (row.shape[0], LANES))
        got = None
        for b in range(blocks):
            piece = jnp.take_along_axis(row[:, b * LANES : (b + 1) * LANES], inside, axis=1, mode="promise_in_bounds")
            got = piece if b == 0 else jnp.where(want // LANES == b, piece, got)
        out.append(got)
    return jnp.concatenate(out, axis=1)


def column_of(row, rows, count):
    if count < rows:
        row = jnp.concatenate([row, jnp.zeros((1, rows - count), row.dtype)], axis=1)
    across = lax.broadcasted_iota(jnp.int32, (rows, rows), 1)
    down = lax.broadcasted_iota(jnp.int32, (rows, rows), 0)
    square = jnp.where(across == down, jnp.broadcast_to(row, (rows, rows)), 0.0)
    return jnp.sum(square, axis=1, keepdims=True)


def total(x, weights):
    x = x * weights
    out = x[:8]
    for r in range(8, x.shape[0], 8):
        out = out + x[r : r + 8]
    return jnp.sum(out, axis=0, keepdims=True)


def column_kernel(*refs, count, elem_size, group_size):
    ins, refs = refs[:count], refs[count:]
    kelvin_ref, moist_ref, diox_ref, depth_ref, slot_ref, share_ref, skin_ref, albedo_ref = ins[:8]
    sun_ref, routes_ref, angles_ref, thermal_ref, sunlight_ref, planck_ref, solar_ref = ins[8:]
    flux_ref, net_lw, depths, shares_ref, depth_out = refs[:5]
    table, passing, downs, rows, warm, edge, sides, fluxes = refs[5:]
    layers, columns = kelvin_ref.shape
    lw, terms = thermal_ref.shape
    sw = sunlight_ref.shape[0]
    nodes = terms // 2
    lw_rows, sw_rows, node_rows = up_to(lw, 16), up_to(sw, 16), up_to(nodes, 16)
    both = lw_rows + sw_rows
    me_elem = lax.axis_index("elem")

    table[...] = jnp.zeros_like(table)
    for first, ref, size in ((0, thermal_ref, lw), (lw_rows, sunlight_ref, sw)):
        values = ref[...]
        for kind in range(2):
            here = values[:, kind * nodes : (kind + 1) * nodes]
            for pair in range(2):
                at = (2 * pair + kind) * node_rows
                table[pair * both + first : pair * both + first + size, at : at + nodes] = here

    planck_row = planck_ref[...].reshape(1, lw)
    solar_row = solar_ref[...].reshape(1, sw)
    pieces = [planck_row, jnp.zeros((1, lw_rows - lw), F32), solar_row, jnp.zeros((1, sw_rows - sw), F32)]
    shares_ref[...] = jnp.concatenate([p for p in pieces if p.shape[1]], axis=1)
    planck = column_of(planck_row, lw_rows, lw)
    solar = column_of(solar_row, sw_rows, sw)

    share = share_ref[...]
    rows[0] = slot_ref[...].astype(F32)
    rows[1] = (1.0 - share) * moist_ref[...]
    rows[2] = (1.0 - share) * diox_ref[...]
    rows[3] = share * moist_ref[...]
    rows[4] = share * diox_ref[...]
    relative = kelvin_ref[...] * (1.0 / 250.0)
    relative = relative * relative
    relative = relative * relative
    warm[...] = relative
    edge[0 : layers - 1] = relative[: layers - 1] - relative[1:]
    edge[layers - 1 : layers] = relative[layers - 1 :]

    angles = angles_ref[...].reshape(1, angles_ref.shape[0])
    bins = angles.shape[1]
    if bins % LANES:
        angles = jnp.concatenate([angles, jnp.zeros((1, up_to(bins, LANES) - bins), F32)], axis=1)
    sun = sun_ref[...].reshape(1, columns)
    angles = jnp.broadcast_to(angles, (8, angles.shape[1]))
    cosine = jnp.where(sun < bins, pick(angles, jnp.minimum(sun, angles.shape[1] - 1))[:1], 0.0)
    skin = skin_ref[...].reshape(1, columns) * (1.0 / 250.0)
    skin = skin * skin
    sides[0:1] = skin * skin
    albedo = albedo_ref[...].reshape(1, columns)
    slant = (-LOG2E) / jnp.where(cosine > 0.0, cosine, 1.0)
    for i, side in enumerate((cosine, slant, albedo)):
        depth_out[layers + i : layers + i + 1] = side

    node_of_row = lax.broadcasted_iota(jnp.int32, (node_rows, columns), 0).astype(F32).astype(BF16)
    node_below = node_of_row - jnp.asarray(1.0, BF16)
    zero = jnp.zeros((node_rows, columns), BF16)

    def spread(kind, l):
        row = jnp.broadcast_to(rows[kind, l : l + 1, :], (16, columns)).astype(BF16)
        return jnp.concatenate([row] * (node_rows // 16), axis=0)

    down = jnp.broadcast_to(-warm[0:1, :], (lw_rows, columns))
    depth = jnp.zeros((sw_rows, columns), F32)
    for l in range(layers):
        if l % 2 == 0:
            amounts = []
            for at in (l, l + 1):
                node = spread(0, at)
                lower, upper = node_of_row == node, node_below == node
                for kind in (1, 2):
                    rest = jnp.where(upper, spread(kind + 2, at), zero)
                    amounts.append(jnp.where(lower, spread(kind, at), rest))
            pair = jnp.dot(table[...], jnp.concatenate(amounts, axis=0), preferred_element_type=F32)
        tau = pair[l % 2 * both : (l % 2 + 1) * both]
        through = jnp.exp2(DIFFUSE * tau[:lw_rows])
        passed = through * down
        passing[l] = through
        downs[l] = down
        down = passed + edge[l : l + 1]
        tau = tau[lw_rows:]
        depths[l] = tau
        depth = depth + tau
    up = jnp.broadcast_to(sides[0:1, :], (lw_rows, columns))
    net_lw[layers] = up - down
    up = up - warm[layers - 1 : layers, :]
    beam = jnp.exp2(slant * depth)
    fluxes[0:1, :] = total(down, planck)
    fluxes[2:3, :] = total(beam, solar)
    fluxes[3:4, :] = total(albedo * beam * jnp.exp2(DIFFUSE * depth), solar)
    for l in reversed(range(layers)):
        passed = passing[l] * up
        net_lw[l] = passed - downs[l]
        up = passed - edge[l - 1 : l, :] if l else passed + warm[0:1, :]
    fluxes[1:2, :] = total(up, planck)


    depth_out[0:layers] = depth_ref[...]
    row = lax.broadcasted_iota(jnp.int32, (8, columns), 0)
    routed = pick(fluxes[...] * jnp.where(row < 2, 1.0, cosine), routes_ref[...].reshape(1, columns))
    peer = columns // elem_size
    share_count = LANES // peer
    lane = lax.broadcasted_iota(jnp.int32, (8, LANES), 1)
    mine = lane // peer == lax.rem(me_elem, share_count)
    for k in range(elem_size):
        piece = routed[:, k // share_count * LANES : (k // share_count + 1) * LANES]
        shift = lax.rem(me_elem + (elem_size * share_count - k), share_count) * peer
        moved = jnp.where(mine, pltpu.roll(piece, shift, 1), 0.0)
        for q in range(group_size):
            flux_ref[k * group_size + q] = moved[q : q + 1]


def heat_kernel(net_lw, depths, shares_ref, depth_ref, *rest):
    heat_refs, heat, falls = rest[:-2], rest[-2], rest[-1]
    group_size = len(heat_refs)
    faces, lw_rows, columns = net_lw.shape
    layers = faces - 1
    both = shares_ref.shape[1]
    per = layers // group_size
    me_gpt = lax.axis_index("gpt")
    shares = jnp.broadcast_to(jnp.concatenate([shares_ref[...]] * per, axis=1), (2 * per, per * both))
    lane = lax.broadcasted_iota(jnp.int32, shares.shape, 1)
    wanted = lax.div(lane, both) + jnp.where(lax.rem(lane, both) < lw_rows, 0, per)
    shares = jnp.where(lax.broadcasted_iota(jnp.int32, shares.shape, 0) == wanted, shares, 0.0)
    high = shares.astype(BF16).astype(F32)
    weights = jnp.concatenate([high, shares - high], axis=0).astype(BF16)
    inverse = 1.0 / depth_ref[0:layers]
    cosine, slant, albedo = (depth_ref[layers + i : layers + i + 1] for i in range(3))
    beam = jnp.ones(depths.shape[1:], F32)
    for l in range(layers):
        passed = beam * jnp.exp2(slant * depths[l])
        falls[l] = beam - passed
        beam = passed
    back = albedo * beam
    for q in reversed(range(group_size)):
        gains = []
        for l in reversed(range(q * per, (q + 1) * per)):
            passed = back * jnp.exp2(DIFFUSE * depths[l])
            gains.append(((back - passed) + falls[l]).astype(BF16))
            gains.append((net_lw[l + 1] - net_lw[l]).astype(BF16))
            back = passed
        gains.reverse()
        sums = jnp.dot(weights, jnp.concatenate(gains, axis=0), preferred_element_type=F32)
        scale = inverse[q * per : (q + 1) * per]
        scale = jnp.concatenate([scale, scale * cosine], axis=0)
        heat[q] = (sums[: 2 * per] + sums[2 * per :]) * scale
    for d in range(group_size):
        heat_refs[d][...] = heat[jnp.bitwise_xor(me_gpt, d)]


def sum_kernel(*refs):
    heats, (lw_ref, sw_ref) = refs[:-2], refs[-2:]
    total = heats[0][...]
    for ref in heats[1:]:
        total = total + ref[...]
    per = lw_ref.shape[0]
    lw_ref[...] = total[:per]
    sw_ref[...] = total[per:]


def flux_kernel(flux_ref, out_ref):
    blocks = out_ref.shape[1] // LANES
    count = flux_ref.shape[0] // blocks
    for b in range(blocks):
        piece = flux_ref[b * count : (b + 1) * count].reshape(count, LANES)
        out_ref[:, b * LANES : (b + 1) * LANES] = jnp.sum(piece, axis=0, keepdims=True)


def local(*args):
    layers, columns = args[0].shape
    lw, terms = args[11].shape
    sw = args[12].shape[0]
    group_size, elem_size = lax.axis_size("gpt"), lax.axis_size("elem")
    lw_rows, sw_rows, node_rows = up_to(lw, 16), up_to(sw, 16), up_to(terms // 2, 16)
    per = layers // group_size
    both = lw_rows + sw_rows
    vmem = pl.BlockSpec(memory_space=pltpu.VMEM)

    def out(*shape):
        return jax.ShapeDtypeStruct(shape, F32)

    flux, *states = pl.pallas_call(
        functools.partial(column_kernel, count=len(args), elem_size=elem_size, group_size=group_size),
        out_shape=[
            out(elem_size * group_size, 1, LANES),
            out(layers + 1, lw_rows, columns),
            out(layers, sw_rows, columns),
            out(1, both),
            out(layers + 8, columns),
        ],
        in_specs=[vmem] * len(args),
        out_specs=[vmem] * 5,
        scratch_shapes=[
            pltpu.VMEM((2 * both, 4 * node_rows), BF16),
            pltpu.VMEM((layers, lw_rows, columns), F32),
            pltpu.VMEM((layers, lw_rows, columns), F32),
            pltpu.VMEM((5, layers, columns), F32),
            pltpu.VMEM((layers, columns), F32),
            pltpu.VMEM((layers, columns), F32),
            pltpu.VMEM((8, columns), F32),
            pltpu.VMEM((8, columns), F32),
        ],
        compiler_params=pltpu.CompilerParams(vmem_limit_bytes=24 << 20),
        name="columns",
    )(*[pltpu.with_memory_space_constraint(a, pltpu.HBM) for a in args])
    heats = pl.pallas_call(
        heat_kernel,
        out_shape=[out(2 * per, columns)] * group_size,
        in_specs=[vmem] * len(states),
        out_specs=[vmem] * group_size,
        scratch_shapes=[
            pltpu.VMEM((group_size, 2 * per, columns), F32),
            pltpu.VMEM((layers, sw_rows, columns), F32),
        ],
        compiler_params=pltpu.CompilerParams(vmem_limit_bytes=8 << 20),
        name="heat",
    )(*states)
    moved = [heats[0]]
    for d in range(1, group_size):
        moved.append(lax.ppermute(heats[d], "gpt", [(i, i ^ d) for i in range(group_size)]))
    flux = lax.all_to_all(flux, ("elem", "gpt"), 0, 0, tiled=True)
    small = pltpu.CompilerParams(vmem_limit_bytes=2 << 20)
    heat_lw, heat_sw = pl.pallas_call(
        sum_kernel,
        out_shape=[out(per, columns)] * 2,
        in_specs=[vmem] * group_size,
        out_specs=[vmem] * 2,
        compiler_params=small,
        name="sums",
    )(*moved)
    surface_flux = pl.pallas_call(
        flux_kernel,
        out_shape=out(1, columns),
        in_specs=[vmem],
        out_specs=vmem,
        compiler_params=small,
        name="spans",
    )(flux)
    return heat_lw, heat_sw, surface_flux


def solution(mesh):
    in_specs = (P(None, "elem"),) * 6 + (P("elem"),) * 4 + (P(), P("gpt", None), P("gpt", None), P("gpt"), P("gpt"))
    out_specs = (P("gpt", "elem"), P("gpt", "elem"), P("gpt", "elem"))
    return jax.shard_map(local, mesh=mesh, in_specs=in_specs, out_specs=out_specs, check_vma=False)
```

```python
import functools

import jax
import jax.numpy as jnp
from jax import lax
from jax.experimental import pallas as pl
from jax.experimental.pallas import tpu as pltpu
from jax.sharding import PartitionSpec as P

F32 = jnp.float32
BF16 = jnp.bfloat16
LANES = 128
LOG2E = 1.4426950408889634
DIFFUSE = -1.66 * LOG2E


def up_to(count, step):
    return (count + step - 1) // step * step


def pick(row, index):
    blocks = row.shape[1] // LANES
    out = []
    for at in range(index.shape[1] // LANES):
        want = index[:, at * LANES : (at + 1) * LANES]
        inside = jnp.broadcast_to(want % LANES, (row.shape[0], LANES))
        got = None
        for b in range(blocks):
            piece = jnp.take_along_axis(row[:, b * LANES : (b + 1) * LANES], inside, axis=1, mode="promise_in_bounds")
            got = piece if b == 0 else jnp.where(want // LANES == b, piece, got)
        out.append(got)
    return jnp.concatenate(out, axis=1)


def column_of(row, rows, count):
    if count < rows:
        row = jnp.concatenate([row, jnp.zeros((1, rows - count), row.dtype)], axis=1)
    across = lax.broadcasted_iota(jnp.int32, (rows, rows), 1)
    down = lax.broadcasted_iota(jnp.int32, (rows, rows), 0)
    square = jnp.where(across == down, jnp.broadcast_to(row, (rows, rows)), 0.0)
    return jnp.sum(square, axis=1, keepdims=True)


def total(x, weights):
    x = x * weights
    out = x[:8]
    for r in range(8, x.shape[0], 8):
        out = out + x[r : r + 8]
    return jnp.sum(out, axis=0, keepdims=True)


def column_kernel(*refs, count, elem_size, group_size):
    ins, refs = refs[:count], refs[count:]
    kelvin_ref, moist_ref, diox_ref, depth_ref, slot_ref, share_ref, skin_ref, albedo_ref = ins[:8]
    sun_ref, routes_ref, angles_ref, thermal_ref, sunlight_ref, planck_ref, solar_ref = ins[8:]
    flux_ref, net_lw, depths, shares_ref, depth_out = refs[:5]
    table, passing, downs, rows, warm, edge, sides, fluxes = refs[5:]
    layers, columns = kelvin_ref.shape
    lw, terms = thermal_ref.shape
    sw = sunlight_ref.shape[0]
    nodes = terms // 2
    lw_rows, sw_rows, node_rows = up_to(lw, 16), up_to(sw, 16), up_to(nodes, 16)
    both = lw_rows + sw_rows
    me_elem = lax.axis_index("elem")

    table[...] = jnp.zeros_like(table)
    for first, ref, size in ((0, thermal_ref, lw), (lw_rows, sunlight_ref, sw)):
        values = ref[...]
        for kind in range(2):
            here = values[:, kind * nodes : (kind + 1) * nodes]
            for pair in range(2):
                at = (2 * pair + kind) * node_rows
                table[pair * both + first : pair * both + first + size, at : at + nodes] = here

    planck_row = planck_ref[...].reshape(1, lw)
    solar_row = solar_ref[...].reshape(1, sw)
    pieces = [planck_row, jnp.zeros((1, lw_rows - lw), F32), solar_row, jnp.zeros((1, sw_rows - sw), F32)]
    shares_ref[...] = jnp.concatenate([p for p in pieces if p.shape[1]], axis=1)
    planck = column_of(planck_row, lw_rows, lw)
    solar = column_of(solar_row, sw_rows, sw)

    routes = routes_ref[...].reshape(1, columns)
    peer = columns // elem_size
    share_count = LANES // peer
    lane = lax.broadcasted_iota(jnp.int32, (8, LANES), 1)
    mine = lane // peer == lax.rem(me_elem, share_count)
    wants = []
    for k in range(elem_size):
        piece = routes[:, k // share_count * LANES : (k // share_count + 1) * LANES]
        shift = lax.rem(me_elem + (elem_size * share_count - k), share_count) * peer
        wants.append(pltpu.roll(jnp.broadcast_to(piece, (8, LANES)), shift, 1))

    share = share_ref[...]
    rows[0] = slot_ref[...].astype(F32)
    rows[1] = (1.0 - share) * moist_ref[...]
    rows[2] = (1.0 - share) * diox_ref[...]
    rows[3] = share * moist_ref[...]
    rows[4] = share * diox_ref[...]
    relative = kelvin_ref[...] * (1.0 / 250.0)
    relative = relative * relative
    relative = relative * relative
    warm[...] = relative
    edge[0 : layers - 1] = relative[: layers - 1] - relative[1:]
    edge[layers - 1 : layers] = relative[layers - 1 :]

    angles = angles_ref[...].reshape(1, angles_ref.shape[0])
    bins = angles.shape[1]
    if bins % LANES:
        angles = jnp.concatenate([angles, jnp.zeros((1, up_to(bins, LANES) - bins), F32)], axis=1)
    sun = sun_ref[...].reshape(1, columns)
    angles = jnp.broadcast_to(angles, (8, angles.shape[1]))
    cosine = jnp.where(sun < bins, pick(angles, jnp.minimum(sun, angles.shape[1] - 1))[:1], 0.0)
    skin = skin_ref[...].reshape(1, columns) * (1.0 / 250.0)
    skin = skin * skin
    sides[0:1] = skin * skin
    albedo = albedo_ref[...].reshape(1, columns)
    slant = (-LOG2E) / jnp.where(cosine > 0.0, cosine, 1.0)
    for i, side in enumerate((cosine, slant, albedo)):
        depth_out[layers + i : layers + i + 1] = side

    node_of_row = lax.broadcasted_iota(jnp.int32, (node_rows, columns), 0).astype(F32).astype(BF16)
    node_below = node_of_row - jnp.asarray(1.0, BF16)
    zero = jnp.zeros((node_rows, columns), BF16)

    def spread(kind, l):
        row = jnp.broadcast_to(rows[kind, l : l + 1, :], (16, columns)).astype(BF16)
        return jnp.concatenate([row] * (node_rows // 16), axis=0)

    down = jnp.broadcast_to(-warm[0:1, :], (lw_rows, columns))
    depth = jnp.zeros((sw_rows, columns), F32)
    for l in range(layers):
        if l % 2 == 0:
            amounts = []
            for at in (l, l + 1):
                node = spread(0, at)
                lower, upper = node_of_row == node, node_below == node
                for kind in (1, 2):
                    rest = jnp.where(upper, spread(kind + 2, at), zero)
                    amounts.append(jnp.where(lower, spread(kind, at), rest))
            pair = jnp.dot(table[...], jnp.concatenate(amounts, axis=0), preferred_element_type=F32)
        tau = pair[l % 2 * both : (l % 2 + 1) * both]
        through = jnp.exp2(DIFFUSE * tau[:lw_rows])
        passed = through * down
        passing[l] = through
        downs[l] = down
        down = passed + edge[l : l + 1]
        tau = tau[lw_rows:]
        depths[l] = tau
        depth = depth + tau
    up = jnp.broadcast_to(sides[0:1, :], (lw_rows, columns))
    net_lw[layers] = up - down
    up = up - warm[layers - 1 : layers, :]
    beam = jnp.exp2(slant * depth)
    fluxes[0:1, :] = total(down, planck)
    fluxes[2:3, :] = total(beam, solar)
    fluxes[3:4, :] = total(albedo * beam * jnp.exp2(DIFFUSE * depth), solar)
    for l in reversed(range(layers)):
        passed = passing[l] * up
        net_lw[l] = passed - downs[l]
        up = passed - edge[l - 1 : l, :] if l else passed + warm[0:1, :]
    fluxes[1:2, :] = total(up, planck)


    depth_out[0:layers] = depth_ref[...]
    row = lax.broadcasted_iota(jnp.int32, (8, columns), 0)
    scaled = fluxes[...] * jnp.where(row < 2, 1.0, cosine)
    for k, want in enumerate(wants):
        moved = jnp.where(mine, pick(scaled, want), 0.0)
        for q in range(group_size):
            flux_ref[k * group_size + q] = moved[q : q + 1]


def heat_kernel(net_lw, depths, shares_ref, depth_ref, *rest):
    heat_refs, heat, falls = rest[:-2], rest[-2], rest[-1]
    group_size = len(heat_refs)
    faces, lw_rows, columns = net_lw.shape
    layers = faces - 1
    both = shares_ref.shape[1]
    per = layers // group_size
    me_gpt = lax.axis_index("gpt")
    shares = jnp.broadcast_to(jnp.concatenate([shares_ref[...]] * per, axis=1), (2 * per, per * both))
    lane = lax.broadcasted_iota(jnp.int32, shares.shape, 1)
    wanted = lax.div(lane, both) + jnp.where(lax.rem(lane, both) < lw_rows, 0, per)
    shares = jnp.where(lax.broadcasted_iota(jnp.int32, shares.shape, 0) == wanted, shares, 0.0)
    high = shares.astype(BF16).astype(F32)
    weights = jnp.concatenate([high, shares - high], axis=0).astype(BF16)
    inverse = 1.0 / depth_ref[0:layers]
    cosine, slant, albedo = (depth_ref[layers + i : layers + i + 1] for i in range(3))
    beam = jnp.ones(depths.shape[1:], F32)
    for l in range(layers):
        passed = beam * jnp.exp2(slant * depths[l])
        falls[l] = beam - passed
        beam = passed
    back = albedo * beam
    for q in reversed(range(group_size)):
        gains = []
        for l in reversed(range(q * per, (q + 1) * per)):
            passed = back * jnp.exp2(DIFFUSE * depths[l])
            gains.append(((back - passed) + falls[l]).astype(BF16))
            gains.append((net_lw[l + 1] - net_lw[l]).astype(BF16))
            back = passed
        gains.reverse()
        sums = jnp.dot(weights, jnp.concatenate(gains, axis=0), preferred_element_type=F32)
        scale = inverse[q * per : (q + 1) * per]
        scale = jnp.concatenate([scale, scale * cosine], axis=0)
        heat[q] = (sums[: 2 * per] + sums[2 * per :]) * scale
    for d in range(group_size):
        heat_refs[d][...] = heat[jnp.bitwise_xor(me_gpt, d)]


def sum_kernel(*refs, group_size):
    heats = refs[:group_size]
    flux_ref, lw_ref, sw_ref, out_ref = refs[group_size:]
    total = heats[0][...]
    for ref in heats[1:]:
        total = total + ref[...]
    per = lw_ref.shape[0]
    lw_ref[...] = total[:per]
    sw_ref[...] = total[per:]
    blocks = out_ref.shape[1] // LANES
    count = flux_ref.shape[0] // blocks
    for b in range(blocks):
        piece = flux_ref[b * count : (b + 1) * count].reshape(count, LANES)
        out_ref[:, b * LANES : (b + 1) * LANES] = jnp.sum(piece, axis=0, keepdims=True)


def local(*args):
    layers, columns = args[0].shape
    lw, terms = args[11].shape
    sw = args[12].shape[0]
    group_size, elem_size = lax.axis_size("gpt"), lax.axis_size("elem")
    lw_rows, sw_rows, node_rows = up_to(lw, 16), up_to(sw, 16), up_to(terms // 2, 16)
    per = layers // group_size
    both = lw_rows + sw_rows
    vmem = pl.BlockSpec(memory_space=pltpu.VMEM)

    def out(*shape):
        return jax.ShapeDtypeStruct(shape, F32)

    flux, *states = pl.pallas_call(
        functools.partial(column_kernel, count=len(args), elem_size=elem_size, group_size=group_size),
        out_shape=[
            out(elem_size * group_size, 1, LANES),
            out(layers + 1, lw_rows, columns),
            out(layers, sw_rows, columns),
            out(1, both),
            out(layers + 8, columns),
        ],
        in_specs=[vmem] * len(args),
        out_specs=[vmem] * 5,
        scratch_shapes=[
            pltpu.VMEM((2 * both, 4 * node_rows), BF16),
            pltpu.VMEM((layers, lw_rows, columns), F32),
            pltpu.VMEM((layers, lw_rows, columns), F32),
            pltpu.VMEM((5, layers, columns), F32),
            pltpu.VMEM((layers, columns), F32),
            pltpu.VMEM((layers, columns), F32),
            pltpu.VMEM((8, columns), F32),
            pltpu.VMEM((8, columns), F32),
        ],
        compiler_params=pltpu.CompilerParams(vmem_limit_bytes=24 << 20),
        name="columns",
    )(*[pltpu.with_memory_space_constraint(a, pltpu.HBM) for a in args])
    heats = pl.pallas_call(
        heat_kernel,
        out_shape=[out(2 * per, columns)] * group_size,
        in_specs=[vmem] * len(states),
        out_specs=[vmem] * group_size,
        scratch_shapes=[
            pltpu.VMEM((group_size, 2 * per, columns), F32),
            pltpu.VMEM((layers, sw_rows, columns), F32),
        ],
        compiler_params=pltpu.CompilerParams(vmem_limit_bytes=8 << 20),
        name="heat",
    )(*states)
    moved = [heats[0]]
    for d in range(1, group_size):
        moved.append(lax.ppermute(heats[d], "gpt", [(i, i ^ d) for i in range(group_size)]))
    flux = lax.all_to_all(flux, ("elem", "gpt"), 0, 0, tiled=True)
    return tuple(
        pl.pallas_call(
            functools.partial(sum_kernel, group_size=group_size),
            out_shape=[
                jax.ShapeDtypeStruct((per, columns), F32),
                jax.ShapeDtypeStruct((per, columns), F32),
                jax.ShapeDtypeStruct((1, columns), F32),
            ],
            in_specs=[vmem] * (group_size + 1),
            out_specs=[vmem] * 3,
            compiler_params=pltpu.CompilerParams(vmem_limit_bytes=2 << 20),
            name="sums",
        )(*moved, flux)
    )


def solution(mesh):
    in_specs = (P(None, "elem"),) * 6 + (P("elem"),) * 4 + (P(), P("gpt", None), P("gpt", None), P("gpt"), P("gpt"))
    out_specs = (P("gpt", "elem"), P("gpt", "elem"), P("gpt", "elem"))
    return jax.shard_map(local, mesh=mesh, in_specs=in_specs, out_specs=out_specs, check_vma=False)
```
